128 devices in a mesh: slab: 4 (over z_hi, core), wide: 32 (over x, z_lo, y).
Axes of the slice: x: 4, y: 4, z: 4 (z_hi: 2, z_lo: 2; z = z_hi * 2 + z_lo), core: 2. Of those that a mesh axis runs over, the one named last changes fastest.
Arguments:
- orbitals: float32 [256, 128, 128, 128], P(None, 'slab', 'wide'), may hold values from -6 to 6
- points: int32 [512], replicated, may hold values from 0 to 2097151, as said below
Outputs:
- potential: float32 [128, 128, 128, 128], P(None, 'slab', 'wide')
The draws below stay inside these ranges and needn't reach their ends.
Inputs may be any that keep to these rules, and one draw needn't show every extreme that they name: `points`: the 512 indices are distinct; how many fall in the cells of one device differs strongly between devices.
All inputs are finite; a program needn't handle non-finite values.
Results may differ from the reference program's by a relative error of at most 0.00014.
Values sent between devices are 32-bit elements; how exact they have to be, the bound alone decides.
No kernel may reach another device: no remote copies, remote signals or barrier semaphores. Data moves between devices by JAX's collectives and lax.ppermute only.
A program may use at most 192 MiB of HBM per device.

```python
import math
import jax
import jax.numpy as jnp
from jax import lax

NG = 128
ORB = 256
NPTS = 512
VEC = 128
CZ = 32
CY = 4
CELLS = 16384


def draw_points(key, part):
    first, second = jax.random.split(key, 2)
    wide_count = NG // CY
    device_count = NG // CZ * wide_count
    factors = jax.random.randint(first, (2, NPTS - 2), 0, device_count)
    owner = factors[0] * factors[1] // device_count
    owner = jnp.concatenate([jnp.array([device_count - 1, 0], jnp.int32), owner.astype(jnp.int32)])
    shuffled = jax.random.permutation(second, CELLS - 2)[:NPTS - 2] + 1
    offset = jnp.concatenate([jnp.array([CELLS - 1, 0], jnp.int32), shuffled.astype(jnp.int32)])
    slab_pos = owner // wide_count
    wide_pos = owner % wide_count
    local_z = offset // (CY * NG)
    local_y = offset // NG % CY
    local_x = offset % NG
    zcoord = slab_pos * CZ + local_z
    ycoord = wide_pos * CY + local_y
    return ((zcoord * NG + ycoord) * NG + local_x).astype(jnp.int32)


def level_of(own_key, dims, cuts, least, largest):
    loudness, own = 1.0, jax.random.fold_in(own_key, 6)
    for axis_at, shards_of in cuts:
        steps = jnp.exp(jax.random.uniform(jax.random.fold_in(own, axis_at), (shards_of,), jnp.float32, least / len(cuts), largest / len(cuts)))
        loudness = loudness * jnp.repeat(steps, dims[axis_at] // shards_of).reshape([-1 if axis == axis_at else 1 for axis in range(len(dims))])
    return loudness


def normal_values(key, dims, spread, most, cuts=(), kind=jnp.bfloat16):
    values = spread * jax.random.normal(key, dims, jnp.float32)
    if cuts:
        values = values * level_of(key, dims, cuts, -0.22, 0.18)
    return jnp.clip(values, -most, most).astype(kind)


def setup_inputs(seed: int = 0) -> dict:
    arg_keys = jax.random.split(jax.random.key(seed), 3)
    orbitals = normal_values(arg_keys[0], (ORB, NG, NG, NG), 1.0, 6.0, ((1, 4), (2, 32)), jnp.float32)
    points = draw_points(jax.random.fold_in(arg_keys[2], 71), 0)
    return {"orbitals": orbitals, "points": points}


highest = lax.Precision.HIGHEST

def coulomb(zfreq, yfreq, xfreq, length, factor):

    def squared(index):
        signed = jnp.where(index > length // 2, index - length, index).astype(jnp.float32) * (2.0 * math.pi / length)
        return signed * signed
    total = squared(zfreq)[:, None, None] + squared(yfreq)[None, :, None] + squared(xfreq)[None, None, :]
    safe = jnp.where(total > 0, total, 1.0)
    return jnp.where(total > 0, 4.0 * math.pi * factor / safe, 0.0)

def reference(orbitals, points):
    flat = orbitals.reshape(ORB, NG * NG * NG)
    sampled = jnp.take(flat, points, axis=1)
    correlation = jnp.dot(sampled.T, sampled, precision=highest)
    gram = correlation * correlation
    gram = gram + 0.01 * jnp.mean(jnp.diagonal(gram)) * jnp.eye(NPTS, dtype=jnp.float32)
    factor = jnp.linalg.cholesky(gram)
    coeffs = jax.scipy.linalg.cho_solve((factor, True), jnp.eye(NPTS, VEC, dtype=jnp.float32))

    def plane_fit(zindex):
        block = lax.dynamic_slice_in_dim(orbitals, zindex, 1, axis=1).reshape(ORB, NG * NG)
        pairs = jnp.dot(sampled.T, block, precision=highest)
        return jnp.dot(coeffs.T, pairs * pairs, precision=highest)
    fitted = lax.map(plane_fit, jnp.arange(NG, dtype=jnp.int32))
    fitting = jnp.transpose(fitted, (1, 0, 2)).reshape(VEC, NG, NG, NG)
    freqs = jnp.arange(NG, dtype=jnp.int32)
    kernel = coulomb(freqs, freqs, freqs, NG, 1.0)
    spectrum = jnp.fft.fftn(fitting, axes=(1, 2, 3))
    return jnp.real(jnp.fft.ifftn(spectrum * kernel, axes=(1, 2, 3))).astype(jnp.float32)
```

```python
import math

import jax
import jax.numpy as jnp
from jax import lax
from jax.sharding import PartitionSpec as P

AXES = ("slab", "wide")
highest = lax.Precision.HIGHEST
high = lax.Precision.HIGH


def hartley(length):
    index = jnp.arange(length, dtype=jnp.int32)
    phase = index[:, None] * index[None, :] % length
    angle = phase.astype(jnp.float32) * (2.0 * math.pi / length)
    return jnp.cos(angle) + jnp.sin(angle)


def coulomb(length, factor):
    index = jnp.arange(length, dtype=jnp.int32)
    signed = jnp.where(index > length // 2, index - length, index).astype(jnp.float32) * (
        2.0 * math.pi / length
    )
    squared = signed * signed
    total = squared[:, None, None] + squared[None, :, None] + squared[None, None, :]
    safe = jnp.where(total > 0, total, 1.0)
    return jnp.where(total > 0, 4.0 * math.pi * factor / safe, 0.0)


def exchange(blocks):
    return lax.all_to_all(blocks, AXES, split_axis=0, concat_axis=0, tiled=True)


def per_device(orbitals, points):
    norbit, depth, rows, grid = orbitals.shape
    npoint = points.shape[0]
    slab_count = lax.axis_size("slab")
    wide_count = lax.axis_size("wide")
    slab_index = lax.axis_index("slab")
    wide_index = lax.axis_index("wide")
    devices = slab_count * wide_count
    vectors = devices
    cells = depth * rows * grid
    flat = orbitals.reshape(norbit, cells)
    zcoord = points // (grid * grid)
    ycoord = points // grid % grid
    xcoord = points % grid
    owned = (zcoord // depth == slab_index) & (ycoord // rows == wide_index)
    offset = ((zcoord - slab_index * depth) * rows + (ycoord - wide_index * rows)) * grid + xcoord
    offset = jnp.where(owned, offset, 0)
    picked = jnp.take(flat, offset, axis=1) * owned.astype(jnp.float32)[None, :]
    mine = exchange(picked.T.reshape(devices, npoint // devices, norbit)).sum(0)
    sampled_rows = exchange(jnp.broadcast_to(mine[None], (devices,) + mine.shape))
    sampled_rows = sampled_rows.reshape(npoint, norbit)
    correlation = jnp.dot(sampled_rows, sampled_rows.T, precision=highest)
    gram = correlation * correlation
    gram = gram + 0.01 * jnp.mean(jnp.diagonal(gram)) * jnp.eye(npoint, dtype=jnp.float32)
    factor = jnp.linalg.cholesky(gram)
    coeffs = jax.scipy.linalg.cho_solve((factor, True), jnp.eye(npoint, vectors, dtype=jnp.float32))
    coeff_rows = coeffs.T
    width = math.gcd(cells, 4096)

    def fit_block(turn, fitted):
        start = turn * width
        block = lax.dynamic_slice_in_dim(flat, start, width, 1)
        pairs = jnp.dot(sampled_rows, block, precision=high)
        piece = jnp.dot(coeff_rows, pairs * pairs, precision=high)
        return lax.dynamic_update_slice_in_dim(fitted, piece, start, 1)

    fitting = lax.fori_loop(0, cells // width, fit_block, jnp.zeros((vectors, cells), jnp.float32))
    whole = exchange(fitting.reshape(vectors, depth, rows, grid))
    whole = whole.reshape(slab_count, wide_count, depth, rows, grid)
    xtab = hartley(grid)
    ytab = xtab.reshape(wide_count, rows, grid)
    ztab = xtab.reshape(slab_count, depth, grid)
    spec = jnp.einsum("swzyx,xk->swzyk", whole, xtab, precision=high)
    spec = jnp.einsum("swzyk,wyq->szqk", spec, ytab, precision=high)
    spec = jnp.einsum("szqk,szp->pqk", spec, ztab, precision=high)
    spec = spec * coulomb(grid, 1.0 / float(grid * grid * grid))
    spec = jnp.einsum("pqk,szp->szqk", spec, ztab, precision=high)
    spec = jnp.einsum("szqk,wyq->swzyk", spec, ytab, precision=high)
    spec = jnp.einsum("swzyk,xk->swzyx", spec, xtab, precision=high)
    return exchange(spec.reshape(devices, depth, rows, grid))


def solution(mesh):
    placed = (P(None, "slab", "wide", None), P())
    return jax.shard_map(
        per_device,
        mesh=mesh,
        in_specs=placed,
        out_specs=P(None, "slab", "wide", None),
        check_vma=False,
    )
```

```python
import functools
import math

import jax
import jax.numpy as jnp
from jax import lax
from jax.experimental import pallas as pl
from jax.experimental.pallas import tpu as pltpu
from jax.sharding import PartitionSpec as P

AXES = ("slab", "wide")
HI = lax.Precision.HIGHEST
BLK = 128
CHUNKS = 2
SLOTS = 8


def hartley(length):
    index = jnp.arange(length, dtype=jnp.int32)
    phase = index[:, None] * index[None, :] % length
    angle = phase.astype(jnp.float32) * (2.0 * math.pi / length)
    return jnp.cos(angle) + jnp.sin(angle)


def exchange(blocks):
    return lax.all_to_all(blocks, AXES, split_axis=0, concat_axis=0, tiled=True)


def halves(value):
    top = value.astype(jnp.bfloat16)
    return top, (value - top.astype(jnp.float32)).astype(jnp.bfloat16)


def split(value):
    top = lax.reduce_precision(value, exponent_bits=8, mantissa_bits=7)
    return top.astype(jnp.bfloat16), (value - top).astype(jnp.bfloat16)


def mul3(left, right):
    def one(a, b):
        return jnp.dot(a, b, preferred_element_type=jnp.float32)

    return one(left[0], right[0]) + (one(left[1], right[0]) + one(left[0], right[1]))


def whole_spec():
    return pl.BlockSpec(memory_space=pltpu.VMEM)


def pick_kernel(info, orb, out_ref, buf, acc, order, sems):
    npoint = info.shape[1]
    lane = lax.broadcasted_iota(jnp.int32, (acc.shape[0], BLK), 1)
    acc[...] = jnp.zeros_like(acc)

    def collect(m, count):
        order[count] = m
        return count + info[0, m]

    total = lax.fori_loop(0, npoint, collect, 0)

    def copy(i):
        m = order[i]
        slot = i % SLOTS
        return pltpu.make_async_copy(orb.at[:, info[1, m]], buf.at[slot], sems.at[slot])

    @pl.loop(0, jnp.minimum(total, SLOTS - 1))
    def _(i):
        copy(i).start()

    @pl.loop(0, total)
    def _(i):
        @pl.when(i + SLOTS - 1 < total)
        def _():
            copy(i + SLOTS - 1).start()

        copy(i).wait()
        m = order[i]
        slot = i % SLOTS
        line = buf[slot, :, info[2, m], :]
        moved = pltpu.roll(line, (m + BLK - info[3, m]) % BLK, 1)
        spot = pl.multiple_of(m // BLK * BLK, BLK)
        acc[:, pl.ds(spot, BLK)] = jnp.where(lane == m % BLK, moved, acc[:, pl.ds(spot, BLK)])

    out_ref[...] = acc[...].T


def pick(info, orbitals):
    norbit, depth, rows, grid = orbitals.shape
    npoint = info.shape[1]
    return pl.pallas_call(
        pick_kernel,
        out_shape=jax.ShapeDtypeStruct((npoint, norbit), jnp.float32),
        in_specs=[pl.BlockSpec(memory_space=pltpu.SMEM), pl.BlockSpec(memory_space=pl.ANY)],
        out_specs=whole_spec(),
        scratch_shapes=[
            pltpu.VMEM((SLOTS, norbit, rows, grid), jnp.float32),
            pltpu.VMEM((norbit, npoint), jnp.float32),
            pltpu.SMEM((npoint + 1,), jnp.int32),
            pltpu.SemaphoreType.DMA((SLOTS,)),
        ],
        name="pick",
    )(info, orbitals)


def factor_block(tile):
    lane = lax.broadcasted_iota(jnp.int32, (8, BLK), 1)
    sub = lax.broadcasted_iota(jnp.int32, (8, BLK), 0)
    groups = [tile[8 * i : 8 * i + 8, :] for i in range(BLK // 8)]
    for k in range(BLK):
        here, off = k // 8, k % 8
        row = jnp.broadcast_to(groups[here][off : off + 1, :], (8, BLK))
        piv = jnp.broadcast_to(row[:, k : k + 1], (8, BLK))
        inv = 1.0 / piv
        unit = jnp.where(lane == k, 1.0, row)
        scaled = unit * inv
        for i in range(here, BLK // 8):
            g = groups[i]
            col = jnp.broadcast_to(g[:, k : k + 1], (8, BLK))
            if i == here:
                col = jnp.where(sub > off, col, 0.0)
                base = jnp.where((lane == k) & (sub > off), 0.0, g)
            else:
                base = jnp.where(lane == k, 0.0, g)
            groups[i] = base - col * scaled
    return jnp.concatenate(groups, axis=0)

def coeff_kernel(s_ref, out_ref, g_ref, p_ref, l_ref):
    n = s_ref.shape[0]
    nb = n // BLK
    rows = s_ref[...]
    corr = lax.dot_general(rows, rows, (((1,), (1,)), ((), ())), precision=HI, preferred_element_type=jnp.float32)
    gram = corr * corr
    r = lax.broadcasted_iota(jnp.int32, (n, n), 0)
    c = lax.broadcasted_iota(jnp.int32, (n, n), 1)
    mean = jnp.sum(jnp.where(r == c, gram, 0.0)) * (1.0 / n)
    g_ref[...] = gram + jnp.where(r == c, 0.01 * mean, 0.0)
    rr = lax.broadcasted_iota(jnp.int32, (BLK, BLK), 0)
    cc = lax.broadcasted_iota(jnp.int32, (BLK, BLK), 1)

    def step(t, carry):
        start = pl.multiple_of((nb - 1 - t) * BLK, BLK)
        tile = factor_block(g_ref[pl.ds(start, BLK), pl.ds(start, BLK)])
        diag = jnp.sum(jnp.where(rr == cc, tile, 0.0), axis=1, keepdims=True)
        low = jnp.where(cc < rr, tile, jnp.where(rr == cc, 1.0, 0.0)) * lax.rsqrt(diag)
        l_ref[pl.ds(start, BLK), :] = low
        panel = jnp.dot(low, g_ref[pl.ds(start, BLK), :], precision=HI, preferred_element_type=jnp.float32)
        p_ref[pl.ds(start, BLK), :] = panel

        @pl.when(t < nb - 1)
        def _():
            g_ref[...] -= lax.dot_general(panel, panel, (((0,), (0,)), ((), ())), precision=HI, preferred_element_type=jnp.float32)
        return carry

    lax.fori_loop(0, nb, step, 0)
    first = l_ref[0:BLK, :]
    out_ref[:, 0:BLK] = lax.dot_general(first, first, (((0,), (0,)), ((), ())), precision=HI, preferred_element_type=jnp.float32)
    for b in range(1, nb):
        lo = b * BLK
        part = lax.dot_general(out_ref[:, 0:lo], p_ref[lo : lo + BLK, 0:lo], (((1,), (1,)), ((), ())), precision=HI, preferred_element_type=jnp.float32)
        out_ref[:, lo : lo + BLK] = -jnp.dot(part, l_ref[lo : lo + BLK, :], precision=HI, preferred_element_type=jnp.float32)

def coefficients(rows):
    n = rows.shape[0]
    return pl.pallas_call(
        coeff_kernel,
        out_shape=jax.ShapeDtypeStruct((BLK, n), jnp.float32),
        scratch_shapes=[pltpu.VMEM((n, n), jnp.float32), pltpu.VMEM((n, n), jnp.float32), pltpu.VMEM((n, BLK), jnp.float32)],
        name="coefficients",
    )(rows)


def fit_kernel(sh, sl, ch, cl, orb, out_ref, bh, bl):
    lines = orb.shape[1]
    for r in range(lines):
        top, low = halves(orb[:, r, :])
        bh[:, r * BLK : (r + 1) * BLK] = top
        bl[:, r * BLK : (r + 1) * BLK] = low
    for r in range(0, lines, 4):
        cut = slice(r * BLK, (r + 4) * BLK)
        pairs = mul3((sh[...], sl[...]), (bh[:, cut], bl[:, cut]))
        piece = mul3((ch[...], cl[...]), halves(pairs * pairs))
        for k in range(4):
            out_ref[:, r + k, :] = piece[:, k * BLK : (k + 1) * BLK]


def fit(sampled, coeffs, orbitals, first, count, lines=8):
    norbit, total, grid = orbitals.shape
    vectors, npoint = coeffs[0].shape
    start = first // lines
    return pl.pallas_call(
        fit_kernel,
        out_shape=jax.ShapeDtypeStruct((vectors, count, grid), jnp.float32),
        grid=(count // lines,),
        in_specs=[
            pl.BlockSpec((npoint, norbit), lambda i: (0, 0)),
            pl.BlockSpec((npoint, norbit), lambda i: (0, 0)),
            pl.BlockSpec((vectors, npoint), lambda i: (0, 0)),
            pl.BlockSpec((vectors, npoint), lambda i: (0, 0)),
            pl.BlockSpec((norbit, lines, grid), lambda i: (0, start + i, 0)),
        ],
        out_specs=pl.BlockSpec((vectors, lines, grid), lambda i: (0, i, 0)),
        scratch_shapes=[
            pltpu.VMEM((norbit, lines * grid), jnp.bfloat16),
            pltpu.VMEM((norbit, lines * grid), jnp.bfloat16),
        ],
        cost_estimate=pl.CostEstimate(
            flops=6 * count * grid * npoint * (norbit + vectors),
            transcendentals=0,
            bytes_accessed=4 * count * grid * (norbit + vectors),
        ),
        name="fit",
    )(*sampled, *coeffs, orbitals)


def planes_in_kernel(xh, xl, yh, yl, in_ref, out_ref):
    for pair in range(in_ref.shape[2] // 8):
        tile = in_ref[0, :, 8 * pair : 8 * pair + 8, :].reshape(2 * BLK, BLK)
        along = mul3(halves(tile), (xh[...], xl[...]))
        both = mul3((yh[...], yl[...]), halves(along))
        out_ref[0, 2 * pair] = both[:BLK]
        out_ref[0, 2 * pair + 1] = both[BLK:]


def planes_out_kernel(xh, xl, yh, yl, in_ref, out_ref):
    for pair in range(in_ref.shape[1] // 2):
        tile = jnp.concatenate([in_ref[0, 2 * pair], in_ref[0, 2 * pair + 1]], axis=0)
        both = mul3((yh[...], yl[...]), halves(tile))
        along = mul3(halves(both), (xh[...], xl[...]))
        out_ref[0, :, 8 * pair : 8 * pair + 8, :] = along.reshape(32, 8, BLK)


def planes(kernel, xtab, ytab, values, out_shape, name, step=8):
    slabs, depth = (values.shape[0], values.shape[2] // 4) if name == "planes_in" else values.shape[:2]
    cellwise = pl.BlockSpec((1, 32, 4 * step, BLK), lambda s, i: (s, 0, i, 0))
    planewise = pl.BlockSpec((1, step, BLK, BLK), lambda s, i: (s, i, 0, 0))
    small = pl.BlockSpec((BLK, BLK), lambda s, i: (0, 0))
    large = pl.BlockSpec((2 * BLK, 2 * BLK), lambda s, i: (0, 0))
    inward = name == "planes_in"
    return pl.pallas_call(
        kernel,
        out_shape=jax.ShapeDtypeStruct(out_shape, jnp.float32),
        grid=(slabs, depth // step),
        in_specs=[small, small, large, large, cellwise if inward else planewise],
        out_specs=planewise if inward else cellwise,
        cost_estimate=pl.CostEstimate(
            flops=6 * values.size * 3 * BLK, transcendentals=0, bytes_accessed=8 * values.size
        ),
        name=name,
    )(*xtab, *ytab, values)


def columns_kernel(count, zh, zl, *refs):
    ins, outs = refs[:count], refs[count:]
    lines = ins[0].shape[1]
    base = pl.program_id(0) * lines
    length = BLK
    unit = 2.0 * math.pi / length

    def square(index):
        signed = jnp.where(index > length // 2, index - length, index).astype(jnp.float32) * unit
        return signed * signed

    zsq = square(lax.broadcasted_iota(jnp.int32, (BLK, BLK), 0))
    xsq = square(lax.broadcasted_iota(jnp.int32, (BLK, BLK), 1))
    flat = zsq + xsq
    part = BLK // count
    for j in range(0, lines, 2):
        tile = jnp.concatenate(
            [
                jnp.concatenate([ref[:, j, :] for ref in ins], axis=0),
                jnp.concatenate([ref[:, j + 1, :] for ref in ins], axis=0),
            ],
            axis=1,
        )
        spec = mul3((zh[0], zl[0]), halves(tile))
        weights = []
        for k in range(2):
            index = base + j + k
            total = flat + square(jnp.full((BLK, BLK), index, jnp.int32))
            safe = jnp.where(total > 0, total, 1.0)
            scale = 4.0 * math.pi / float(length**3)
            weights.append(jnp.where(total > 0, scale / safe, 0.0))
        spec = spec * jnp.concatenate(weights, axis=1)
        back = mul3((zh[1], zl[1]), halves(spec))
        for c, ref in enumerate(outs):
            for k in range(2):
                ref[:, j + k, :] = back[c * part : (c + 1) * part, k * BLK : (k + 1) * BLK]


def columns(ztab, values, lines=8):
    count = len(values)
    part = BLK // count
    spec = pl.BlockSpec((part, lines, BLK), lambda i: (0, i, 0))
    table = pl.BlockSpec((2, BLK, BLK), lambda i: (0, 0, 0))
    size = BLK**3
    return pl.pallas_call(
        functools.partial(columns_kernel, count),
        out_shape=[jax.ShapeDtypeStruct((part, BLK, BLK), jnp.float32)] * count,
        grid=(BLK // lines,),
        in_specs=[table, table] + [spec] * count,
        out_specs=[spec] * count,
        cost_estimate=pl.CostEstimate(
            flops=12 * size * BLK, transcendentals=size, bytes_accessed=8 * size
        ),
        name="columns",
    )(*ztab, *values)


def per_device(orbitals, points):
    norbit, depth, rows, grid = orbitals.shape
    npoint = points.shape[0]
    slabs = lax.axis_size("slab")
    wides = lax.axis_size("wide")
    slab_index = lax.axis_index("slab")
    wide_index = lax.axis_index("wide")
    devices = slabs * wides
    zcoord = points // (grid * grid)
    ycoord = points // grid % grid
    xcoord = points % grid
    owned = (zcoord // depth == slab_index) & (ycoord // rows == wide_index)
    info = jnp.stack([owned.astype(jnp.int32), zcoord % depth, ycoord % rows, xcoord])
    picked = pick(info, orbitals)
    mine = exchange(picked.reshape(devices, npoint // devices, norbit)).sum(0)
    sampled_rows = exchange(jnp.broadcast_to(mine[None], (devices,) + mine.shape))
    sampled_rows = sampled_rows.reshape(npoint, norbit)
    coeffs = split(coefficients(sampled_rows))
    sampled = split(sampled_rows)

    table = hartley(grid)
    xtab = split(table)
    part = depth // CHUNKS
    lines = table.reshape(grid, wides, 1, rows)
    eye = jnp.eye(2, dtype=jnp.float32)
    ysplit = (eye[:, None, None, :, None] * lines[None]).reshape(2 * grid, wides * 2 * rows)
    ztable = table.reshape(grid, slabs, CHUNKS, part).transpose(0, 2, 1, 3).reshape(grid, grid)
    yin, yout = split(ysplit), split(ysplit.T)
    ztab = split(jnp.stack([ztable, ztable.T]))

    flat = orbitals.reshape(norbit, depth * rows, grid)
    spectra = []
    for c in range(CHUNKS):
        piece = fit(sampled, coeffs, flat, c * part * rows, part * rows)
        whole = exchange(piece).reshape(slabs, wides, part * rows, grid)
        spec = planes(planes_in_kernel, xtab, yin, whole, (slabs, part, grid, grid), "planes_in")
        spectra.append(spec.reshape(slabs * part, grid, grid))
    spectra = columns(ztab, spectra)
    out = []
    for c in range(CHUNKS):
        spec = spectra[c].reshape(slabs, part, grid, grid)
        back = planes(planes_out_kernel, xtab, yout, spec, (slabs, wides, part * rows, grid), "planes_out")
        out.append(exchange(back.reshape(devices, part * rows, grid)).reshape(devices, part, rows, grid))
    return jnp.concatenate(out, axis=1)


def solution(mesh):
    placed = (P(None, "slab", "wide", None), P())
    return jax.shard_map(
        per_device,
        mesh=mesh,
        in_specs=placed,
        out_specs=P(None, "slab", "wide", None),
        check_vma=False,
    )
```

```python
import functools
import math

import jax
import jax.numpy as jnp
from jax import lax
from jax.experimental import pallas as pl
from jax.experimental.pallas import tpu as pltpu
from jax.sharding import PartitionSpec as P

AXES = ("slab", "wide")
HI = lax.Precision.HIGHEST
BLK = 128
PARTS = (8, 16, 8)
SLOTS = 8


def hartley(length):
    index = jnp.arange(length, dtype=jnp.int32)
    phase = index[:, None] * index[None, :] % length
    angle = phase.astype(jnp.float32) * (2.0 * math.pi / length)
    return jnp.cos(angle) + jnp.sin(angle)


def exchange(blocks):
    return lax.all_to_all(blocks, AXES, split_axis=0, concat_axis=0, tiled=True)


def halves(value):
    top = value.astype(jnp.bfloat16)
    return top, (value - top.astype(jnp.float32)).astype(jnp.bfloat16)


def split(value):
    top = lax.reduce_precision(value, exponent_bits=8, mantissa_bits=7)
    return top.astype(jnp.bfloat16), (value - top).astype(jnp.bfloat16)


def mul3(left, right):
    def one(a, b):
        return jnp.dot(a, b, preferred_element_type=jnp.float32)

    return one(left[0], right[0]) + (one(left[1], right[0]) + one(left[0], right[1]))


def whole_spec():
    return pl.BlockSpec(memory_space=pltpu.VMEM)


def pick_kernel(info, orb, out_ref, buf, acc, order, sems):
    npoint = info.shape[1]
    lane = lax.broadcasted_iota(jnp.int32, (acc.shape[0], BLK), 1)
    acc[...] = jnp.zeros_like(acc)

    def collect(m, count):
        order[count] = m
        return count + info[0, m]

    total = lax.fori_loop(0, npoint, collect, 0)

    def copy(i):
        m = order[i]
        slot = i % SLOTS
        return pltpu.make_async_copy(orb.at[:, info[1, m]], buf.at[slot], sems.at[slot])

    @pl.loop(0, jnp.minimum(total, SLOTS - 1))
    def _(i):
        copy(i).start()

    @pl.loop(0, total)
    def _(i):
        @pl.when(i + SLOTS - 1 < total)
        def _():
            copy(i + SLOTS - 1).start()

        copy(i).wait()
        m = order[i]
        slot = i % SLOTS
        line = buf[slot, :, info[2, m], :]
        moved = pltpu.roll(line, (m + BLK - info[3, m]) % BLK, 1)
        spot = pl.multiple_of(m // BLK * BLK, BLK)
        acc[:, pl.ds(spot, BLK)] = jnp.where(lane == m % BLK, moved, acc[:, pl.ds(spot, BLK)])

    out_ref[...] = acc[...].T


def pick(info, orbitals):
    norbit, depth, rows, grid = orbitals.shape
    npoint = info.shape[1]
    return pl.pallas_call(
        pick_kernel,
        out_shape=jax.ShapeDtypeStruct((npoint, norbit), jnp.float32),
        in_specs=[pl.BlockSpec(memory_space=pltpu.SMEM), pl.BlockSpec(memory_space=pl.ANY)],
        out_specs=whole_spec(),
        scratch_shapes=[
            pltpu.VMEM((SLOTS, norbit, rows, grid), jnp.float32),
            pltpu.VMEM((norbit, npoint), jnp.float32),
            pltpu.SMEM((npoint + 1,), jnp.int32),
            pltpu.SemaphoreType.DMA((SLOTS,)),
        ],
        name="pick",
    )(info, orbitals)


def factor_block(tile):
    lane = lax.broadcasted_iota(jnp.int32, (8, BLK), 1)
    sub = lax.broadcasted_iota(jnp.int32, (8, BLK), 0)
    groups = [tile[8 * i : 8 * i + 8, :] for i in range(BLK // 8)]
    for k in range(BLK):
        here, off = k // 8, k % 8
        row = jnp.broadcast_to(groups[here][off : off + 1, :], (8, BLK))
        piv = jnp.broadcast_to(row[:, k : k + 1], (8, BLK))
        inv = 1.0 / piv
        unit = jnp.where(lane == k, 1.0, row)
        scaled = unit * inv
        for i in range(here, BLK // 8):
            g = groups[i]
            col = jnp.broadcast_to(g[:, k : k + 1], (8, BLK))
            if i == here:
                col = jnp.where(sub > off, col, 0.0)
                base = jnp.where((lane == k) & (sub > off), 0.0, g)
            else:
                base = jnp.where(lane == k, 0.0, g)
            groups[i] = base - col * scaled
    return jnp.concatenate(groups, axis=0)

def coeff_kernel(s_ref, ch_ref, cl_ref, sh_ref, sl_ref, out_ref, g_ref, p_ref, l_ref):
    n = s_ref.shape[0]
    nb = n // BLK
    rows = s_ref[...]
    sh_ref[...], sl_ref[...] = halves(rows)
    corr = lax.dot_general(rows, rows, (((1,), (1,)), ((), ())), precision=HI, preferred_element_type=jnp.float32)
    gram = corr * corr
    r = lax.broadcasted_iota(jnp.int32, (n, n), 0)
    c = lax.broadcasted_iota(jnp.int32, (n, n), 1)
    mean = jnp.sum(jnp.where(r == c, gram, 0.0)) * (1.0 / n)
    g_ref[...] = gram + jnp.where(r == c, 0.01 * mean, 0.0)
    rr = lax.broadcasted_iota(jnp.int32, (BLK, BLK), 0)
    cc = lax.broadcasted_iota(jnp.int32, (BLK, BLK), 1)

    def step(t, carry):
        start = pl.multiple_of((nb - 1 - t) * BLK, BLK)
        tile = factor_block(g_ref[pl.ds(start, BLK), pl.ds(start, BLK)])
        diag = jnp.sum(jnp.where(rr == cc, tile, 0.0), axis=1, keepdims=True)
        low = jnp.where(cc < rr, tile, jnp.where(rr == cc, 1.0, 0.0)) * lax.rsqrt(diag)
        l_ref[pl.ds(start, BLK), :] = low
        panel = jnp.dot(low, g_ref[pl.ds(start, BLK), :], precision=HI, preferred_element_type=jnp.float32)
        p_ref[pl.ds(start, BLK), :] = panel

        @pl.when(t < nb - 1)
        def _():
            g_ref[...] -= lax.dot_general(panel, panel, (((0,), (0,)), ((), ())), precision=HI, preferred_element_type=jnp.float32)
        return carry

    lax.fori_loop(0, nb, step, 0)
    first = l_ref[0:BLK, :]
    out_ref[:, 0:BLK] = lax.dot_general(first, first, (((0,), (0,)), ((), ())), precision=HI, preferred_element_type=jnp.float32)
    for b in range(1, nb):
        lo = b * BLK
        part = lax.dot_general(out_ref[:, 0:lo], p_ref[lo : lo + BLK, 0:lo], (((1,), (1,)), ((), ())), precision=HI, preferred_element_type=jnp.float32)
        out_ref[:, lo : lo + BLK] = -jnp.dot(part, l_ref[lo : lo + BLK, :], precision=HI, preferred_element_type=jnp.float32)
    ch_ref[...], cl_ref[...] = halves(out_ref[...])


def coefficients(rows):
    n, width = rows.shape
    coeff = jax.ShapeDtypeStruct((BLK, n), jnp.bfloat16)
    sample = jax.ShapeDtypeStruct((n, width), jnp.bfloat16)
    ch, cl, sh, sl = pl.pallas_call(
        coeff_kernel,
        out_shape=[coeff, coeff, sample, sample],
        scratch_shapes=[
            pltpu.VMEM((BLK, n), jnp.float32),
            pltpu.VMEM((n, n), jnp.float32),
            pltpu.VMEM((n, n), jnp.float32),
            pltpu.VMEM((n, BLK), jnp.float32),
        ],
        name="coefficients",
    )(rows)
    return (ch, cl), (sh, sl)


def fit_kernel(sh, sl, ch, cl, orb, out_ref, bh, bl):
    lines = orb.shape[1]
    turned = jnp.transpose(orb[...], (1, 0, 2))
    for r in range(lines):
        top, low = halves(turned[r])
        bh[:, r * BLK : (r + 1) * BLK] = top
        bl[:, r * BLK : (r + 1) * BLK] = low
    pairs = mul3((sh[...], sl[...]), (bh[...], bl[...]))
    piece = mul3((ch[...], cl[...]), halves(pairs * pairs))
    piece = jnp.stack([piece[:, r * BLK : (r + 1) * BLK] for r in range(lines)], axis=0)
    out_ref[...] = jnp.transpose(piece, (1, 0, 2))


def fit(sampled, coeffs, orbitals, first, count, lines=8):
    norbit, total, grid = orbitals.shape
    vectors, npoint = coeffs[0].shape
    start = first // lines
    return pl.pallas_call(
        fit_kernel,
        out_shape=jax.ShapeDtypeStruct((vectors, count, grid), jnp.float32),
        grid=(count // lines,),
        in_specs=[
            pl.BlockSpec((npoint, norbit), lambda i: (0, 0)),
            pl.BlockSpec((npoint, norbit), lambda i: (0, 0)),
            pl.BlockSpec((vectors, npoint), lambda i: (0, 0)),
            pl.BlockSpec((vectors, npoint), lambda i: (0, 0)),
            pl.BlockSpec((norbit, lines, grid), lambda i: (0, start + i, 0)),
        ],
        out_specs=pl.BlockSpec((vectors, lines, grid), lambda i: (0, i, 0)),
        scratch_shapes=[
            pltpu.VMEM((norbit, lines * grid), jnp.bfloat16),
            pltpu.VMEM((norbit, lines * grid), jnp.bfloat16),
        ],
        cost_estimate=pl.CostEstimate(
            flops=6 * count * grid * npoint * (norbit + vectors),
            transcendentals=0,
            bytes_accessed=4 * count * grid * (norbit + vectors),
        ),
        name="fit",
    )(*sampled, *coeffs, orbitals)


def planes_in_kernel(xh, xl, yh, yl, in_ref, out_ref):
    pairs = in_ref.shape[2] // 8
    for p in range(0, pairs, 4):
        tall = [in_ref[0, :, 8 * (p + g) : 8 * (p + g) + 8, :].reshape(2 * BLK, BLK) for g in range(4)]
        along = mul3(halves(jnp.concatenate(tall, axis=0)), (xh[...], xl[...]))
        wide = [along[2 * BLK * g : 2 * BLK * (g + 1)] for g in range(4)]
        both = mul3((yh[...], yl[...]), halves(jnp.concatenate(wide, axis=1)))
        for g in range(4):
            out_ref[0, 2 * (p + g)] = both[:BLK, BLK * g : BLK * (g + 1)]
            out_ref[0, 2 * (p + g) + 1] = both[BLK:, BLK * g : BLK * (g + 1)]


def planes_out_kernel(xh, xl, yh, yl, in_ref, out_ref):
    pairs = in_ref.shape[1] // 2
    wide = [in_ref[0, 2 * g : 2 * g + 2].reshape(2 * BLK, BLK) for g in range(pairs)]
    both = mul3((yh[...], yl[...]), halves(jnp.concatenate(wide, axis=1)))
    tall = [both[:, BLK * g : BLK * (g + 1)] for g in range(pairs)]
    along = mul3(halves(jnp.concatenate(tall, axis=0)), (xh[...], xl[...]))
    for g in range(pairs):
        out_ref[0, :, 8 * g : 8 * g + 8, :] = along[2 * BLK * g : 2 * BLK * (g + 1)].reshape(32, 8, BLK)


def planes(kernel, xtab, ytab, values, out_shape, name):
    inward = name == "planes_in"
    slabs, depth = (values.shape[0], values.shape[2] // 4) if inward else values.shape[:2]
    cellwise = pl.BlockSpec((1, 32, 4 * depth, BLK), lambda s: (s, 0, 0, 0))
    planewise = pl.BlockSpec((1, depth, BLK, BLK), lambda s: (s, 0, 0, 0))
    small = pl.BlockSpec((BLK, BLK), lambda s: (0, 0))
    large = pl.BlockSpec((2 * BLK, 2 * BLK), lambda s: (0, 0))
    return pl.pallas_call(
        kernel,
        out_shape=jax.ShapeDtypeStruct(out_shape, jnp.float32),
        grid=(slabs,),
        in_specs=[small, small, large, large, cellwise if inward else planewise],
        out_specs=planewise if inward else cellwise,
        cost_estimate=pl.CostEstimate(
            flops=6 * values.size * 3 * BLK, transcendentals=0, bytes_accessed=8 * values.size
        ),
        name=name,
    )(*xtab, *ytab, values)


def columns_kernel(count, zh, zl, *refs):
    ins, outs = refs[:count], refs[count:]
    lines = ins[0].shape[1]
    base = pl.program_id(0) * lines
    length = BLK
    unit = 2.0 * math.pi / length

    def square(index):
        signed = jnp.where(index > length // 2, index - length, index).astype(jnp.float32) * unit
        return signed * signed

    zsq = square(lax.broadcasted_iota(jnp.int32, (BLK, BLK), 0))
    xsq = square(lax.broadcasted_iota(jnp.int32, (BLK, BLK), 1))
    flat = zsq + xsq
    tile = jnp.concatenate([jnp.transpose(ref[...], (1, 0, 2)) for ref in ins], axis=1)
    spec = mul3((zh[0], zl[0]), halves(jnp.concatenate([tile[j] for j in range(lines)], axis=1)))
    scale = 4.0 * math.pi / float(length**3)
    weights = []
    for j in range(lines):
        total = flat + square(jnp.full((BLK, BLK), base + j, jnp.int32))
        safe = jnp.where(total > 0, total, 1.0)
        weights.append(jnp.where(total > 0, scale / safe, 0.0))
    spec = spec * jnp.concatenate(weights, axis=1)
    back = mul3((zh[1], zl[1]), halves(spec))
    back = jnp.stack([back[:, j * BLK : (j + 1) * BLK] for j in range(lines)], axis=0)
    start = 0
    for ref in outs:
        part = ref.shape[0]
        ref[...] = jnp.transpose(back[:, start : start + part], (1, 0, 2))
        start += part


def columns(ztab, values, lines=8):
    count = len(values)
    specs = [pl.BlockSpec((v.shape[0], lines, BLK), lambda i: (0, i, 0)) for v in values]
    table = pl.BlockSpec((2, BLK, BLK), lambda i: (0, 0, 0))
    size = BLK**3
    return pl.pallas_call(
        functools.partial(columns_kernel, count),
        out_shape=[jax.ShapeDtypeStruct(v.shape, jnp.float32) for v in values],
        grid=(BLK // lines,),
        in_specs=[table, table] + specs,
        out_specs=specs,
        cost_estimate=pl.CostEstimate(
            flops=12 * size * BLK, transcendentals=size, bytes_accessed=8 * size
        ),
        name="columns",
    )(*ztab, *values)


def join_kernel(first, src, *refs):
    out, sems = refs[-2], refs[-1]
    quarter = src.shape[0] // 4
    copies = [
        pltpu.make_async_copy(
            src.at[pl.ds(k * quarter, quarter)],
            out.at[pl.ds(k * quarter, quarter), pl.ds(first, src.shape[1])],
            sems.at[k],
        )
        for k in range(4)
    ]
    for copy in copies:
        copy.start()
    for copy in copies:
        copy.wait()


def join(piece, whole, first, shape):
    anywhere = pl.BlockSpec(memory_space=pl.ANY)
    args = (piece,) if whole is None else (piece, whole)
    return pl.pallas_call(
        functools.partial(join_kernel, first),
        out_shape=jax.ShapeDtypeStruct(shape, jnp.float32),
        in_specs=[whole_spec()] + [anywhere] * (len(args) - 1),
        out_specs=anywhere,
        input_output_aliases={} if whole is None else {1: 0},
        scratch_shapes=[pltpu.SemaphoreType.DMA((4,))],
        cost_estimate=pl.CostEstimate(flops=0, transcendentals=0, bytes_accessed=8 * piece.size),
        name="join",
    )(*args)


def per_device(orbitals, points):
    norbit, depth, rows, grid = orbitals.shape
    npoint = points.shape[0]
    slabs = lax.axis_size("slab")
    wides = lax.axis_size("wide")
    slab_index = lax.axis_index("slab")
    wide_index = lax.axis_index("wide")
    devices = slabs * wides
    zcoord = points // (grid * grid)
    ycoord = points // grid % grid
    xcoord = points % grid
    owned = (zcoord // depth == slab_index) & (ycoord // rows == wide_index)
    info = jnp.stack([owned.astype(jnp.int32), zcoord % depth, ycoord % rows, xcoord])
    picked = pick(info, orbitals)
    mine = exchange(picked.reshape(devices, npoint // devices, norbit)).sum(0)
    sampled_rows = exchange(jnp.broadcast_to(mine[None], (devices,) + mine.shape))
    sampled_rows = sampled_rows.reshape(npoint, norbit)
    coeffs, sampled = coefficients(sampled_rows)
    table = hartley(grid)
    xtab = split(table)
    lines = table.reshape(grid, wides, 1, rows)
    eye = jnp.eye(2, dtype=jnp.float32)
    ysplit = (eye[:, None, None, :, None] * lines[None]).reshape(2 * grid, wides * 2 * rows)
    starts = [sum(PARTS[:c]) for c in range(len(PARTS))]
    zrows = table.reshape(grid, slabs, depth)
    ztable = jnp.concatenate(
        [zrows[:, :, lo : lo + part].reshape(grid, slabs * part) for lo, part in zip(starts, PARTS)], axis=1
    )
    yin, yout = split(ysplit), split(ysplit.T)
    ztab = split(jnp.stack([ztable, ztable.T]))

    flat = orbitals.reshape(norbit, depth * rows, grid)
    spectra = []
    for lo, part in zip(starts, PARTS):
        piece = fit(sampled, coeffs, flat, lo * rows, part * rows)
        piece, flat = lax.optimization_barrier((piece, flat))
        whole = exchange(piece).reshape(slabs, wides, part * rows, grid)
        spec = planes(planes_in_kernel, xtab, yin, whole, (slabs, part, grid, grid), "planes_in")
        spectra.append(spec.reshape(slabs * part, grid, grid))
    spectra = columns(ztab, spectra)
    out = None
    for spec, lo, part in zip(spectra, starts, PARTS):
        spec = spec.reshape(slabs, part, grid, grid)
        back = planes(planes_out_kernel, xtab, yout, spec, (slabs, wides, part * rows, grid), "planes_out")
        piece = exchange(back.reshape(devices, part * rows, grid)).reshape(devices, part, rows, grid)
        out = join(piece, out, lo, (devices, depth, rows, grid))
    return out


def solution(mesh):
    placed = (P(None, "slab", "wide", None), P())
    return jax.shard_map(
        per_device,
        mesh=mesh,
        in_specs=placed,
        out_specs=P(None, "slab", "wide", None),
        check_vma=False,
    )
```

```python
import functools
import math

import jax
import jax.numpy as jnp
from jax import lax
from jax.experimental import pallas as pl
from jax.experimental.pallas import tpu as pltpu
from jax.sharding import PartitionSpec as P

AXES = ("slab", "wide")
HI = lax.Precision.HIGHEST
BLK = 128
PARTS = (16, 16)
SLOTS = 8
PANEL = 16


def hartley(length):
    index = jnp.arange(length, dtype=jnp.int32)
    phase = index[:, None] * index[None, :] % length
    angle = phase.astype(jnp.float32) * (2.0 * math.pi / length)
    return jnp.cos(angle) + jnp.sin(angle)


def exchange(blocks):
    return lax.all_to_all(blocks, AXES, split_axis=0, concat_axis=0, tiled=True)


def halves(value):
    top = value.astype(jnp.bfloat16)
    return top, (value - top.astype(jnp.float32)).astype(jnp.bfloat16)


def split(value):
    top = lax.reduce_precision(value, exponent_bits=8, mantissa_bits=7)
    return top.astype(jnp.bfloat16), (value - top).astype(jnp.bfloat16)


def mul3(left, right):
    def one(a, b):
        return jnp.dot(a, b, preferred_element_type=jnp.float32)

    return one(left[0], right[0]) + (one(left[1], right[0]) + one(left[0], right[1]))


def left3(high, low, value):
    top = jnp.concatenate([high, high], axis=1)
    bottom = jnp.concatenate([low, jnp.zeros_like(low)], axis=1)
    table = jnp.concatenate([top, bottom], axis=0)
    both = jnp.dot(table, jnp.concatenate(halves(value), axis=0), preferred_element_type=jnp.float32)
    return both[: high.shape[0]] + both[high.shape[0] :]


def whole_spec():
    return pl.BlockSpec(memory_space=pltpu.VMEM)


def pick_kernel(info, orb, out_ref, buf, acc, order, sems):
    npoint = info.shape[1]
    lane = lax.broadcasted_iota(jnp.int32, (acc.shape[0], BLK), 1)
    acc[...] = jnp.zeros_like(acc)

    def collect(m, count):
        order[count] = m
        return count + info[0, m]

    total = lax.fori_loop(0, npoint, collect, 0)

    def copy(i):
        m = order[i]
        slot = i % SLOTS
        return pltpu.make_async_copy(orb.at[:, info[1, m]], buf.at[slot], sems.at[slot])

    @pl.loop(0, jnp.minimum(total, SLOTS - 1))
    def _(i):
        copy(i).start()

    @pl.loop(0, total)
    def _(i):
        @pl.when(i + SLOTS - 1 < total)
        def _():
            copy(i + SLOTS - 1).start()

        copy(i).wait()
        m = order[i]
        slot = i % SLOTS
        line = buf[slot, :, info[2, m], :]
        moved = pltpu.roll(line, (m + BLK - info[3, m]) % BLK, 1)
        spot = pl.multiple_of(m // BLK * BLK, BLK)
        acc[:, pl.ds(spot, BLK)] = jnp.where(lane == m % BLK, moved, acc[:, pl.ds(spot, BLK)])

    out_ref[...] = acc[...].T


def pick(info, orbitals):
    norbit, depth, rows, grid = orbitals.shape
    npoint = info.shape[1]
    return pl.pallas_call(
        pick_kernel,
        out_shape=jax.ShapeDtypeStruct((npoint, norbit), jnp.float32),
        in_specs=[pl.BlockSpec(memory_space=pltpu.SMEM), pl.BlockSpec(memory_space=pl.ANY)],
        out_specs=whole_spec(),
        scratch_shapes=[
            pltpu.VMEM((SLOTS, norbit, rows, grid), jnp.float32),
            pltpu.VMEM((norbit, npoint), jnp.float32),
            pltpu.SMEM((npoint + 1,), jnp.int32),
            pltpu.SemaphoreType.DMA((SLOTS,)),
        ],
        name="pick",
    )(info, orbitals)


def factor_block(tile):
    lane = lax.broadcasted_iota(jnp.int32, (8, BLK), 1)
    sub = lax.broadcasted_iota(jnp.int32, (8, BLK), 0)
    cur = tile
    done, invs = [], []
    for p in range(BLK // PANEL):
        lo = PANEL * p
        inside = (lane >= lo) & (lane < lo + PANEL)
        E = {}
        for i0 in range(0, PANEL, 8):
            R = cur[i0:i0 + 8, :]
            for j in range(min(PANEL, i0 + 8)):
                cj = jnp.broadcast_to(R[:, lo + j : lo + j + 1], (8, BLK))
                for i in range(max(j, i0), i0 + 8):
                    E[i, j] = jnp.broadcast_to(cj[i - i0 : i - i0 + 1, :], (8, BLK))
        rows = [jnp.where(inside, jnp.where(lane == lo + k, 1.0, 0.0), jnp.broadcast_to(cur[k : k + 1, :], (8, BLK))) for k in range(PANEL)]
        U = [jnp.zeros((8, BLK), jnp.float32)] * (PANEL // 8); I = list(U)
        for k in range(PANEL):
            inv = 1.0 / E[k, k]
            g = k // 8
            U[g] = jnp.where(sub == k - 8 * g, rows[k], U[g])
            I[g] = jnp.where(sub == k - 8 * g, inv, I[g])
            ls = {i: E[i, k] * inv for i in range(k + 1, PANEL)}
            for i in range(k + 1, PANEL):
                for j in range(k + 1, i + 1):
                    E[i, j] = E[i, j] - ls[i] * E[j, k]
                rows[i] = rows[i] - ls[i] * rows[k]
        Uc = jnp.concatenate(U, axis=0); Ic = jnp.concatenate(I, axis=0)
        done.append(Uc); invs.append(Ic)
        if p < BLK // PANEL - 1:
            upd = lax.dot_general(Uc, Uc * Ic, (((0,), (0,)), ((), ())), precision=HI, preferred_element_type=jnp.float32)
            rest = cur[PANEL:, :]
            lanes = lax.broadcasted_iota(jnp.int32, rest.shape, 1)
            cur = jnp.where((lanes >= lo) & (lanes < lo + PANEL), 0.0, rest) - upd[lo + PANEL :, :]
    return jnp.concatenate(done, axis=0), jnp.concatenate(invs, axis=0)


def coeff_kernel(s_ref, ch_ref, cl_ref, sh_ref, sl_ref, out_ref, g_ref, p_ref, l_ref):
    n = s_ref.shape[0]
    nb = n // BLK
    rows = s_ref[...]
    sh_ref[...], sl_ref[...] = halves(rows)
    corr = lax.dot_general(rows, rows, (((1,), (1,)), ((), ())), precision=HI, preferred_element_type=jnp.float32)
    gram = corr * corr
    r = lax.broadcasted_iota(jnp.int32, (n, n), 0)
    c = lax.broadcasted_iota(jnp.int32, (n, n), 1)
    mean = jnp.sum(jnp.where(r == c, gram, 0.0)) * (1.0 / n)
    g_ref[...] = gram + jnp.where(r == c, 0.01 * mean, 0.0)
    rr = lax.broadcasted_iota(jnp.int32, (BLK, BLK), 0)
    cc = lax.broadcasted_iota(jnp.int32, (BLK, BLK), 1)

    def step(t, carry):
        start = pl.multiple_of((nb - 1 - t) * BLK, BLK)
        tile, invs = factor_block(g_ref[pl.ds(start, BLK), pl.ds(start, BLK)])
        low = jnp.where(cc <= rr, tile, 0.0) * jnp.sqrt(invs)
        l_ref[pl.ds(start, BLK), :] = low
        panel = jnp.dot(low, g_ref[pl.ds(start, BLK), :], precision=HI, preferred_element_type=jnp.float32)
        p_ref[pl.ds(start, BLK), :] = panel

        @pl.when(t < nb - 1)
        def _():
            g_ref[...] -= lax.dot_general(panel, panel, (((0,), (0,)), ((), ())), precision=HI, preferred_element_type=jnp.float32)
        return carry

    lax.fori_loop(0, nb, step, 0)
    first = l_ref[0:BLK, :]
    out_ref[:, 0:BLK] = lax.dot_general(first, first, (((0,), (0,)), ((), ())), precision=HI, preferred_element_type=jnp.float32)
    for b in range(1, nb):
        lo = b * BLK
        part = lax.dot_general(out_ref[:, 0:lo], p_ref[lo : lo + BLK, 0:lo], (((1,), (1,)), ((), ())), precision=HI, preferred_element_type=jnp.float32)
        out_ref[:, lo : lo + BLK] = -jnp.dot(part, l_ref[lo : lo + BLK, :], precision=HI, preferred_element_type=jnp.float32)
    ch_ref[...], cl_ref[...] = halves(out_ref[...])


def coefficients(rows):
    n, width = rows.shape
    coeff = jax.ShapeDtypeStruct((BLK, n), jnp.bfloat16)
    sample = jax.ShapeDtypeStruct((n, width), jnp.bfloat16)
    ch, cl, sh, sl = pl.pallas_call(
        coeff_kernel,
        out_shape=[coeff, coeff, sample, sample],
        scratch_shapes=[
            pltpu.VMEM((BLK, n), jnp.float32),
            pltpu.VMEM((n, n), jnp.float32),
            pltpu.VMEM((n, n), jnp.float32),
            pltpu.VMEM((n, BLK), jnp.float32),
        ],
        name="coefficients",
    )(rows)
    return (ch, cl), (sh, sl)


def fit_kernel(sh, sl, ch, cl, orb, out_ref, bh, bl):
    lines = orb.shape[1]
    turned = jnp.transpose(orb[...], (1, 0, 2))
    for r in range(lines):
        top, low = halves(turned[r])
        bh[:, r * BLK : (r + 1) * BLK] = top
        bl[:, r * BLK : (r + 1) * BLK] = low
    pairs = mul3((sh[...], sl[...]), (bh[...], bl[...]))
    piece = mul3((ch[...], cl[...]), halves(pairs * pairs))
    piece = jnp.stack([piece[:, r * BLK : (r + 1) * BLK] for r in range(lines)], axis=0)
    out_ref[...] = jnp.transpose(piece, (1, 0, 2))


def fit(sampled, coeffs, orbitals, first, count, lines=8):
    norbit, total, grid = orbitals.shape
    vectors, npoint = coeffs[0].shape
    start = first // lines
    return pl.pallas_call(
        fit_kernel,
        out_shape=jax.ShapeDtypeStruct((vectors, count, grid), jnp.float32),
        grid=(count // lines,),
        in_specs=[
            pl.BlockSpec((npoint, norbit), lambda i: (0, 0)),
            pl.BlockSpec((npoint, norbit), lambda i: (0, 0)),
            pl.BlockSpec((vectors, npoint), lambda i: (0, 0)),
            pl.BlockSpec((vectors, npoint), lambda i: (0, 0)),
            pl.BlockSpec((norbit, lines, grid), lambda i: (0, start + i, 0)),
        ],
        out_specs=pl.BlockSpec((vectors, lines, grid), lambda i: (0, i, 0)),
        scratch_shapes=[
            pltpu.VMEM((norbit, lines * grid), jnp.bfloat16),
            pltpu.VMEM((norbit, lines * grid), jnp.bfloat16),
        ],
        cost_estimate=pl.CostEstimate(
            flops=6 * count * grid * npoint * (norbit + vectors),
            transcendentals=0,
            bytes_accessed=4 * count * grid * (norbit + vectors),
        ),
        name="fit",
    )(*sampled, *coeffs, orbitals)


def planes_in_kernel(xh, xl, yh, yl, in_ref, out_ref):
    pairs = in_ref.shape[2] // 8
    for p in range(0, pairs, 4):
        tall = [in_ref[0, :, 8 * (p + g) : 8 * (p + g) + 8, :].reshape(2 * BLK, BLK) for g in range(4)]
        along = mul3(halves(jnp.concatenate(tall, axis=0)), (xh[...], xl[...]))
        wide = [along[2 * BLK * g : 2 * BLK * (g + 1)] for g in range(4)]
        both = mul3((yh[...], yl[...]), halves(jnp.concatenate(wide, axis=1)))
        for g in range(4):
            out_ref[0, 2 * (p + g)] = both[:BLK, BLK * g : BLK * (g + 1)]
            out_ref[0, 2 * (p + g) + 1] = both[BLK:, BLK * g : BLK * (g + 1)]


def planes_out_kernel(xh, xl, yh, yl, in_ref, out_ref):
    pairs = in_ref.shape[1] // 2
    wide = [in_ref[0, 2 * g : 2 * g + 2].reshape(2 * BLK, BLK) for g in range(pairs)]
    both = mul3((yh[...], yl[...]), halves(jnp.concatenate(wide, axis=1)))
    tall = [both[:, BLK * g : BLK * (g + 1)] for g in range(pairs)]
    along = mul3(halves(jnp.concatenate(tall, axis=0)), (xh[...], xl[...]))
    for g in range(pairs):
        out_ref[0, :, 8 * g : 8 * g + 8, :] = along[2 * BLK * g : 2 * BLK * (g + 1)].reshape(32, 8, BLK)


def planes(kernel, xtab, ytab, values, out_shape, name):
    inward = name == "planes_in"
    slabs, depth = (values.shape[0], values.shape[2] // 4) if inward else values.shape[:2]
    cellwise = pl.BlockSpec((1, 32, 4 * depth, BLK), lambda s: (s, 0, 0, 0))
    planewise = pl.BlockSpec((1, depth, BLK, BLK), lambda s: (s, 0, 0, 0))
    small = pl.BlockSpec((BLK, BLK), lambda s: (0, 0))
    large = pl.BlockSpec((2 * BLK, 2 * BLK), lambda s: (0, 0))
    return pl.pallas_call(
        kernel,
        out_shape=jax.ShapeDtypeStruct(out_shape, jnp.float32),
        grid=(slabs,),
        in_specs=[small, small, large, large, cellwise if inward else planewise],
        out_specs=planewise if inward else cellwise,
        cost_estimate=pl.CostEstimate(
            flops=6 * values.size * 3 * BLK, transcendentals=0, bytes_accessed=8 * values.size
        ),
        name=name,
    )(*xtab, *ytab, values)


def columns_kernel(count, zh, zl, *refs):
    ins, outs = refs[:count], refs[count:]
    lines = ins[0].shape[1]
    base = pl.program_id(0) * lines
    length = BLK
    unit = 2.0 * math.pi / length

    def square(index):
        signed = jnp.where(index > length // 2, index - length, index).astype(jnp.float32) * unit
        return signed * signed

    zsq = square(lax.broadcasted_iota(jnp.int32, (BLK, BLK), 0))
    xsq = square(lax.broadcasted_iota(jnp.int32, (BLK, BLK), 1))
    flat = zsq + xsq
    tile = jnp.concatenate([jnp.transpose(ref[...], (1, 0, 2)) for ref in ins], axis=1)
    spec = left3(zh[0], zl[0], jnp.concatenate([tile[j] for j in range(lines)], axis=1))
    scale = 4.0 * math.pi / float(length**3)
    weights = []
    for j in range(lines):
        total = flat + square(jnp.full((BLK, BLK), base + j, jnp.int32))
        safe = jnp.where(total > 0, total, 1.0)
        weights.append(jnp.where(total > 0, scale / safe, 0.0))
    spec = spec * jnp.concatenate(weights, axis=1)
    back = left3(zh[1], zl[1], spec)
    back = jnp.stack([back[:, j * BLK : (j + 1) * BLK] for j in range(lines)], axis=0)
    start = 0
    for ref in outs:
        part = ref.shape[0]
        ref[...] = jnp.transpose(back[:, start : start + part], (1, 0, 2))
        start += part


def columns(ztab, values, lines=16):
    count = len(values)
    specs = [pl.BlockSpec((v.shape[0], lines, BLK), lambda i: (0, i, 0)) for v in values]
    table = pl.BlockSpec((2, BLK, BLK), lambda i: (0, 0, 0))
    size = BLK**3
    return pl.pallas_call(
        functools.partial(columns_kernel, count),
        out_shape=[jax.ShapeDtypeStruct(v.shape, jnp.float32) for v in values],
        grid=(BLK // lines,),
        in_specs=[table, table] + specs,
        out_specs=specs,
        cost_estimate=pl.CostEstimate(
            flops=12 * size * BLK, transcendentals=size, bytes_accessed=8 * size
        ),
        name="columns",
    )(*ztab, *values)


def join_kernel(first, src, *refs):
    out, sems = refs[-2], refs[-1]
    quarter = src.shape[0] // 4
    copies = [
        pltpu.make_async_copy(
            src.at[pl.ds(k * quarter, quarter)],
            out.at[pl.ds(k * quarter, quarter), pl.ds(first, src.shape[1])],
            sems.at[k],
        )
        for k in range(4)
    ]
    for copy in copies:
        copy.start()
    for copy in copies:
        copy.wait()


def join(piece, whole, first, shape):
    anywhere = pl.BlockSpec(memory_space=pl.ANY)
    args = (piece,) if whole is None else (piece, whole)
    return pl.pallas_call(
        functools.partial(join_kernel, first),
        out_shape=jax.ShapeDtypeStruct(shape, jnp.float32),
        in_specs=[whole_spec()] + [anywhere] * (len(args) - 1),
        out_specs=anywhere,
        input_output_aliases={} if whole is None else {1: 0},
        scratch_shapes=[pltpu.SemaphoreType.DMA((4,))],
        cost_estimate=pl.CostEstimate(flops=0, transcendentals=0, bytes_accessed=8 * piece.size),
        name="join",
    )(*args)


def per_device(orbitals, points):
    norbit, depth, rows, grid = orbitals.shape
    npoint = points.shape[0]
    slabs = lax.axis_size("slab")
    wides = lax.axis_size("wide")
    slab_index = lax.axis_index("slab")
    wide_index = lax.axis_index("wide")
    devices = slabs * wides
    zcoord = points // (grid * grid)
    ycoord = points // grid % grid
    xcoord = points % grid
    owned = (zcoord // depth == slab_index) & (ycoord // rows == wide_index)
    info = jnp.stack([owned.astype(jnp.int32), zcoord % depth, ycoord % rows, xcoord])
    picked = pick(info, orbitals)
    mine = exchange(picked.reshape(devices, npoint // devices, norbit)).sum(0)
    sampled_rows = exchange(jnp.broadcast_to(mine[None], (devices,) + mine.shape))
    sampled_rows = sampled_rows.reshape(npoint, norbit)
    coeffs, sampled = coefficients(sampled_rows)
    table = hartley(grid)
    xtab = split(table)
    lines = table.reshape(grid, wides, 1, rows)
    eye = jnp.eye(2, dtype=jnp.float32)
    ysplit = (eye[:, None, None, :, None] * lines[None]).reshape(2 * grid, wides * 2 * rows)
    starts = [sum(PARTS[:c]) for c in range(len(PARTS))]
    zrows = table.reshape(grid, slabs, depth)
    ztable = jnp.concatenate(
        [zrows[:, :, lo : lo + part].reshape(grid, slabs * part) for lo, part in zip(starts, PARTS)], axis=1
    )
    yin, yout = split(ysplit), split(ysplit.T)
    ztab = split(jnp.stack([ztable, ztable.T]))

    flat = orbitals.reshape(norbit, depth * rows, grid)
    spectra = []
    for lo, part in zip(starts, PARTS):
        piece = fit(sampled, coeffs, flat, lo * rows, part * rows)
        piece, flat = lax.optimization_barrier((piece, flat))
        whole = exchange(piece).reshape(slabs, wides, part * rows, grid)
        spec = planes(planes_in_kernel, xtab, yin, whole, (slabs, part, grid, grid), "planes_in")
        spectra.append(spec.reshape(slabs * part, grid, grid))
    spectra = columns(ztab, spectra)
    out = None
    for spec, lo, part in zip(spectra, starts, PARTS):
        spec = spec.reshape(slabs, part, grid, grid)
        back = planes(planes_out_kernel, xtab, yout, spec, (slabs, wides, part * rows, grid), "planes_out")
        piece = exchange(back.reshape(devices, part * rows, grid)).reshape(devices, part, rows, grid)
        out = join(piece, out, lo, (devices, depth, rows, grid))
    return out


def solution(mesh):
    placed = (P(None, "slab", "wide", None), P())
    return jax.shard_map(
        per_device,
        mesh=mesh,
        in_specs=placed,
        out_specs=P(None, "slab", "wide", None),
        check_vma=False,
    )
```

```python
import functools
import math

import jax
import jax.numpy as jnp
from jax import lax
from jax.experimental import pallas as pl
from jax.experimental.pallas import tpu as pltpu
from jax.sharding import PartitionSpec as P

AXES = ("slab", "wide")
HI = lax.Precision.HIGHEST
BLK = 128
PARTS = (12, 20)
SLOTS = 8
PANEL = 16


def hartley(length):
    index = jnp.arange(length, dtype=jnp.int32)
    phase = index[:, None] * index[None, :] % length
    angle = phase.astype(jnp.float32) * (2.0 * math.pi / length)
    return jnp.cos(angle) + jnp.sin(angle)


def exchange(blocks):
    return lax.all_to_all(blocks, AXES, split_axis=0, concat_axis=0, tiled=True)


def halves(value):
    top = value.astype(jnp.bfloat16)
    return top, (value - top.astype(jnp.float32)).astype(jnp.bfloat16)


def split(value):
    top = lax.reduce_precision(value, exponent_bits=8, mantissa_bits=7)
    return top.astype(jnp.bfloat16), (value - top).astype(jnp.bfloat16)


def mul3(left, right):
    def one(a, b):
        return jnp.dot(a, b, preferred_element_type=jnp.float32)

    return one(left[0], right[0]) + (one(left[1], right[0]) + one(left[0], right[1]))


def stacked3(left, right):
    size = left[0].shape[0]
    both = jnp.dot(jnp.concatenate(left, axis=0), right[0], preferred_element_type=jnp.float32)
    return both[:size] + (both[size:] + jnp.dot(left[0], right[1], preferred_element_type=jnp.float32))


def left3(high, low, value):
    top = jnp.concatenate([high, high], axis=1)
    bottom = jnp.concatenate([low, jnp.zeros_like(low)], axis=1)
    table = jnp.concatenate([top, bottom], axis=0)
    both = jnp.dot(table, jnp.concatenate(halves(value), axis=0), preferred_element_type=jnp.float32)
    return both[: high.shape[0]] + both[high.shape[0] :]


def whole_spec():
    return pl.BlockSpec(memory_space=pltpu.VMEM)


def pick_kernel(info, orb, out_ref, buf, acc, order, sems):
    npoint = info.shape[1]
    lane = lax.broadcasted_iota(jnp.int32, (acc.shape[0], BLK), 1)

    def collect(m, count):
        order[count] = m
        return count + info[0, m]

    total = lax.fori_loop(0, npoint, collect, 0, unroll=16)

    def copy(i):
        m = order[i]
        slot = i % SLOTS
        return pltpu.make_async_copy(orb.at[:, info[1, m]], buf.at[slot], sems.at[slot])

    @pl.loop(0, jnp.minimum(total, SLOTS - 1))
    def _(i):
        copy(i).start()

    acc[...] = jnp.zeros_like(acc)

    @pl.loop(0, total)
    def _(i):
        @pl.when(i + SLOTS - 1 < total)
        def _():
            copy(i + SLOTS - 1).start()

        copy(i).wait()
        m = order[i]
        slot = i % SLOTS
        line = buf[slot, :, info[2, m], :]
        moved = pltpu.roll(line, (m + BLK - info[3, m]) % BLK, 1)
        spot = pl.multiple_of(m // BLK * BLK, BLK)
        acc[:, pl.ds(spot, BLK)] = jnp.where(lane == m % BLK, moved, acc[:, pl.ds(spot, BLK)])

    out_ref[...] = acc[...].T


def pick(info, orbitals):
    norbit, depth, rows, grid = orbitals.shape
    npoint = info.shape[1]
    return pl.pallas_call(
        pick_kernel,
        out_shape=jax.ShapeDtypeStruct((npoint, norbit), jnp.float32),
        in_specs=[pl.BlockSpec(memory_space=pltpu.SMEM), pl.BlockSpec(memory_space=pl.ANY)],
        out_specs=whole_spec(),
        scratch_shapes=[
            pltpu.VMEM((SLOTS, norbit, rows, grid), jnp.float32),
            pltpu.VMEM((norbit, npoint), jnp.float32),
            pltpu.SMEM((npoint + 1,), jnp.int32),
            pltpu.SemaphoreType.DMA((SLOTS,)),
        ],
        name="pick",
    )(info, orbitals)


def factor_block(tile):
    lane = lax.broadcasted_iota(jnp.int32, (8, BLK), 1)
    sub = lax.broadcasted_iota(jnp.int32, (8, BLK), 0)
    cur = tile
    done, invs = [], []
    for p in range(BLK // PANEL):
        lo = PANEL * p
        inside = (lane >= lo) & (lane < lo + PANEL)
        E = {}
        for i0 in range(0, PANEL, 8):
            R = cur[i0:i0 + 8, :]
            for j in range(min(PANEL, i0 + 8)):
                cj = jnp.broadcast_to(R[:, lo + j : lo + j + 1], (8, BLK))
                for i in range(max(j, i0), i0 + 8):
                    E[i, j] = jnp.broadcast_to(cj[i - i0 : i - i0 + 1, :], (8, BLK))
        rows = [jnp.where(inside, jnp.where(lane == lo + k, 1.0, 0.0), jnp.broadcast_to(cur[k : k + 1, :], (8, BLK))) for k in range(PANEL)]
        U = [jnp.zeros((8, BLK), jnp.float32)] * (PANEL // 8); I = list(U)
        for k in range(PANEL):
            inv = 1.0 / E[k, k]
            g = k // 8
            U[g] = jnp.where(sub == k - 8 * g, rows[k], U[g])
            I[g] = jnp.where(sub == k - 8 * g, inv, I[g])
            ls = {i: E[i, k] * inv for i in range(k + 1, PANEL)}
            for i in range(k + 1, PANEL):
                for j in range(k + 1, i + 1):
                    E[i, j] = E[i, j] - ls[i] * E[j, k]
                rows[i] = rows[i] - ls[i] * rows[k]
        Uc = jnp.concatenate(U, axis=0); Ic = jnp.concatenate(I, axis=0)
        done.append(Uc); invs.append(Ic)
        if p < BLK // PANEL - 1:
            upd = lax.dot_general(Uc, Uc * Ic, (((0,), (0,)), ((), ())), precision=HI, preferred_element_type=jnp.float32)
            rest = cur[PANEL:, :]
            lanes = lax.broadcasted_iota(jnp.int32, rest.shape, 1)
            cur = jnp.where((lanes >= lo) & (lanes < lo + PANEL), 0.0, rest) - upd[lo + PANEL :, :]
    return jnp.concatenate(done, axis=0), jnp.concatenate(invs, axis=0)


def coeff_kernel(s_ref, ch_ref, cl_ref, sh_ref, sl_ref, out_ref, g_ref, p_ref, l_ref):
    n = s_ref.shape[0]
    nb = n // BLK
    rows = s_ref[...]
    sh_ref[...], sl_ref[...] = halves(rows)
    corr = lax.dot_general(rows, rows, (((1,), (1,)), ((), ())), precision=HI, preferred_element_type=jnp.float32)
    gram = corr * corr
    r = lax.broadcasted_iota(jnp.int32, (n, n), 0)
    c = lax.broadcasted_iota(jnp.int32, (n, n), 1)
    mean = jnp.sum(jnp.where(r == c, gram, 0.0)) * (1.0 / n)
    g_ref[...] = gram + jnp.where(r == c, 0.01 * mean, 0.0)
    rr = lax.broadcasted_iota(jnp.int32, (BLK, BLK), 0)
    cc = lax.broadcasted_iota(jnp.int32, (BLK, BLK), 1)

    def step(t, carry):
        start = pl.multiple_of((nb - 1 - t) * BLK, BLK)
        tile, invs = factor_block(g_ref[pl.ds(start, BLK), pl.ds(start, BLK)])
        low = jnp.where(cc <= rr, tile, 0.0) * jnp.sqrt(invs)
        l_ref[pl.ds(start, BLK), :] = low
        panel = jnp.dot(low, g_ref[pl.ds(start, BLK), :], precision=HI, preferred_element_type=jnp.float32)
        p_ref[pl.ds(start, BLK), :] = panel

        @pl.when(t < nb - 1)
        def _():
            g_ref[...] -= lax.dot_general(panel, panel, (((0,), (0,)), ((), ())), precision=HI, preferred_element_type=jnp.float32)
        return carry

    lax.fori_loop(0, nb, step, 0)
    first = l_ref[0:BLK, :]
    out_ref[:, 0:BLK] = lax.dot_general(first, first, (((0,), (0,)), ((), ())), precision=HI, preferred_element_type=jnp.float32)
    for b in range(1, nb):
        lo = b * BLK
        part = lax.dot_general(out_ref[:, 0:lo], p_ref[lo : lo + BLK, 0:lo], (((1,), (1,)), ((), ())), precision=HI, preferred_element_type=jnp.float32)
        out_ref[:, lo : lo + BLK] = -jnp.dot(part, l_ref[lo : lo + BLK, :], precision=HI, preferred_element_type=jnp.float32)
    ch_ref[...], cl_ref[...] = halves(out_ref[...])


def coefficients(rows):
    n, width = rows.shape
    coeff = jax.ShapeDtypeStruct((BLK, n), jnp.bfloat16)
    sample = jax.ShapeDtypeStruct((n, width), jnp.bfloat16)
    ch, cl, sh, sl = pl.pallas_call(
        coeff_kernel,
        out_shape=[coeff, coeff, sample, sample],
        scratch_shapes=[
            pltpu.VMEM((BLK, n), jnp.float32),
            pltpu.VMEM((n, n), jnp.float32),
            pltpu.VMEM((n, n), jnp.float32),
            pltpu.VMEM((n, BLK), jnp.float32),
        ],
        name="coefficients",
    )(rows)
    return (ch, cl), (sh, sl)


def fit_kernel(sh, sl, ch, cl, orb, out_ref, bh, bl):
    lines = orb.shape[1]
    turned = jnp.transpose(orb[...], (1, 0, 2))
    for r in range(lines):
        top, low = halves(turned[r])
        bh[:, r * BLK : (r + 1) * BLK] = top
        bl[:, r * BLK : (r + 1) * BLK] = low
    pairs = stacked3((sh[...], sl[...]), (bh[...], bl[...]))
    piece = stacked3((ch[...], cl[...]), halves(pairs * pairs))
    piece = jnp.stack([piece[:, r * BLK : (r + 1) * BLK] for r in range(lines)], axis=0)
    out_ref[...] = jnp.transpose(piece, (1, 0, 2))


def fit(sampled, coeffs, orbitals, first, count, lines=8):
    norbit, total, grid = orbitals.shape
    vectors, npoint = coeffs[0].shape
    start = first // lines
    return pl.pallas_call(
        fit_kernel,
        out_shape=jax.ShapeDtypeStruct((vectors, count, grid), jnp.float32),
        grid=(count // lines,),
        in_specs=[
            pl.BlockSpec((npoint, norbit), lambda i: (0, 0)),
            pl.BlockSpec((npoint, norbit), lambda i: (0, 0)),
            pl.BlockSpec((vectors, npoint), lambda i: (0, 0)),
            pl.BlockSpec((vectors, npoint), lambda i: (0, 0)),
            pl.BlockSpec((norbit, lines, grid), lambda i: (0, start + i, 0)),
        ],
        out_specs=pl.BlockSpec((vectors, lines, grid), lambda i: (0, i, 0)),
        scratch_shapes=[
            pltpu.VMEM((norbit, lines * grid), jnp.bfloat16),
            pltpu.VMEM((norbit, lines * grid), jnp.bfloat16),
        ],
        cost_estimate=pl.CostEstimate(
            flops=6 * count * grid * npoint * (norbit + vectors),
            transcendentals=0,
            bytes_accessed=4 * count * grid * (norbit + vectors),
        ),
        name="fit",
    )(*sampled, *coeffs, orbitals)


def planes_in_kernel(xh, xl, yh, yl, in_ref, out_ref):
    pairs = in_ref.shape[2] // 8
    group = pairs // 2
    for p in range(0, pairs, group):
        tall = [in_ref[0, :, 8 * (p + g) : 8 * (p + g) + 8, :].reshape(2 * BLK, BLK) for g in range(group)]
        along = mul3(halves(jnp.concatenate(tall, axis=0)), (xh[...], xl[...]))
        wide = [along[2 * BLK * g : 2 * BLK * (g + 1)] for g in range(group)]
        both = mul3((yh[...], yl[...]), halves(jnp.concatenate(wide, axis=1)))
        for g in range(group):
            out_ref[0, 2 * (p + g)] = both[:BLK, BLK * g : BLK * (g + 1)]
            out_ref[0, 2 * (p + g) + 1] = both[BLK:, BLK * g : BLK * (g + 1)]


def planes_out_kernel(xh, xl, yh, yl, in_ref, out_ref):
    pairs = in_ref.shape[1] // 2
    wide = [in_ref[0, 2 * g : 2 * g + 2].reshape(2 * BLK, BLK) for g in range(pairs)]
    both = mul3((yh[...], yl[...]), halves(jnp.concatenate(wide, axis=1)))
    tall = [both[:, BLK * g : BLK * (g + 1)] for g in range(pairs)]
    along = mul3(halves(jnp.concatenate(tall, axis=0)), (xh[...], xl[...]))
    for g in range(pairs):
        out_ref[0, :, 8 * g : 8 * g + 8, :] = along[2 * BLK * g : 2 * BLK * (g + 1)].reshape(32, 8, BLK)


def planes(kernel, xtab, ytab, values, out_shape, name):
    inward = name == "planes_in"
    slabs, depth = (values.shape[0], values.shape[2] // 4) if inward else values.shape[:2]
    cellwise = pl.BlockSpec((1, 32, 4 * depth, BLK), lambda s: (s, 0, 0, 0))
    planewise = pl.BlockSpec((1, depth, BLK, BLK), lambda s: (s, 0, 0, 0))
    small = pl.BlockSpec((BLK, BLK), lambda s: (0, 0))
    large = pl.BlockSpec((2 * BLK, 2 * BLK), lambda s: (0, 0))
    return pl.pallas_call(
        kernel,
        out_shape=jax.ShapeDtypeStruct(out_shape, jnp.float32),
        grid=(slabs,),
        in_specs=[small, small, large, large, cellwise if inward else planewise],
        out_specs=planewise if inward else cellwise,
        cost_estimate=pl.CostEstimate(
            flops=6 * values.size * 3 * BLK, transcendentals=0, bytes_accessed=8 * values.size
        ),
        name=name,
    )(*xtab, *ytab, values)


def columns_kernel(start, zh, zl, *refs):
    ins, out = refs[:-1], refs[-1]
    lines = ins[0].shape[1]
    base = pl.program_id(0) * lines
    length = BLK
    unit = 2.0 * math.pi / length

    def square(index):
        signed = jnp.where(index > length // 2, index - length, index).astype(jnp.float32) * unit
        return signed * signed

    zsq = square(lax.broadcasted_iota(jnp.int32, (BLK, BLK), 0))
    xsq = square(lax.broadcasted_iota(jnp.int32, (BLK, BLK), 1))
    flat = zsq + xsq
    tile = jnp.concatenate([jnp.transpose(ref[...], (1, 0, 2)) for ref in ins], axis=1)
    spec = left3(zh[0], zl[0], jnp.concatenate([tile[j] for j in range(lines)], axis=1))
    scale = 4.0 * math.pi / float(length**3)
    weights = []
    for j in range(lines):
        total = flat + square(jnp.full((BLK, BLK), base + j, jnp.int32))
        safe = jnp.where(total > 0, total, 1.0)
        weights.append(jnp.where(total > 0, scale / safe, 0.0))
    spec = spec * jnp.concatenate(weights, axis=1)
    part = out.shape[0]
    back = left3(zh[1, start : start + part], zl[1, start : start + part], spec)
    back = jnp.stack([back[:, j * BLK : (j + 1) * BLK] for j in range(lines)], axis=0)
    out[...] = jnp.transpose(back, (1, 0, 2))


def columns(ztab, values, which, lines=16):
    start = sum(v.shape[0] for v in values[:which])
    specs = [pl.BlockSpec((v.shape[0], lines, BLK), lambda i: (0, i, 0)) for v in values]
    table = pl.BlockSpec((2, BLK, BLK), lambda i: (0, 0, 0))
    size = BLK**3
    return pl.pallas_call(
        functools.partial(columns_kernel, start),
        out_shape=jax.ShapeDtypeStruct(values[which].shape, jnp.float32),
        grid=(BLK // lines,),
        in_specs=[table, table] + specs,
        out_specs=specs[which],
        cost_estimate=pl.CostEstimate(flops=9 * size * BLK, transcendentals=size, bytes_accessed=6 * size),
        name="columns",
    )(*ztab, *values)


def join_kernel(first, src, *refs):
    out, sems = refs[-2], refs[-1]
    quarter = src.shape[0] // 4
    copies = [
        pltpu.make_async_copy(
            src.at[pl.ds(k * quarter, quarter)],
            out.at[pl.ds(k * quarter, quarter), pl.ds(first, src.shape[1])],
            sems.at[k],
        )
        for k in range(4)
    ]
    for copy in copies:
        copy.start()
    for copy in copies:
        copy.wait()


def join(piece, whole, first, shape):
    anywhere = pl.BlockSpec(memory_space=pl.ANY)
    args = (piece,) if whole is None else (piece, whole)
    return pl.pallas_call(
        functools.partial(join_kernel, first),
        out_shape=jax.ShapeDtypeStruct(shape, jnp.float32),
        in_specs=[whole_spec()] + [anywhere] * (len(args) - 1),
        out_specs=anywhere,
        input_output_aliases={} if whole is None else {1: 0},
        scratch_shapes=[pltpu.SemaphoreType.DMA((4,))],
        cost_estimate=pl.CostEstimate(flops=0, transcendentals=0, bytes_accessed=8 * piece.size),
        name="join",
    )(*args)


def per_device(orbitals, points):
    norbit, depth, rows, grid = orbitals.shape
    npoint = points.shape[0]
    slabs = lax.axis_size("slab")
    wides = lax.axis_size("wide")
    slab_index = lax.axis_index("slab")
    wide_index = lax.axis_index("wide")
    devices = slabs * wides
    zcoord = points // (grid * grid)
    ycoord = points // grid % grid
    xcoord = points % grid
    owned = (zcoord // depth == slab_index) & (ycoord // rows == wide_index)
    info = jnp.stack([owned.astype(jnp.int32), zcoord % depth, ycoord % rows, xcoord])
    picked = pick(info, orbitals)
    mine = exchange(picked.reshape(devices, npoint // devices, norbit)).sum(0)
    sampled_rows = exchange(jnp.broadcast_to(mine[None], (devices,) + mine.shape))
    sampled_rows = sampled_rows.reshape(npoint, norbit)
    coeffs, sampled = coefficients(sampled_rows)
    table = hartley(grid)
    xtab = split(table)
    lines = table.reshape(grid, wides, 1, rows)
    eye = jnp.eye(2, dtype=jnp.float32)
    ysplit = (eye[:, None, None, :, None] * lines[None]).reshape(2 * grid, wides * 2 * rows)
    starts = [sum(PARTS[:c]) for c in range(len(PARTS))]
    zrows = table.reshape(grid, slabs, depth)
    ztable = jnp.concatenate(
        [zrows[:, :, lo : lo + part].reshape(grid, slabs * part) for lo, part in zip(starts, PARTS)], axis=1
    )
    yin, yout = split(ysplit), split(ysplit.T)
    ztab = split(jnp.stack([ztable, ztable.T]))

    flat = orbitals.reshape(norbit, depth * rows, grid)
    spectra = []
    for lo, part in zip(starts, PARTS):
        piece = fit(sampled, coeffs, flat, lo * rows, part * rows)
        piece, flat = lax.optimization_barrier((piece, flat))
        whole = exchange(piece).reshape(slabs, wides, part * rows, grid)
        spec = planes(planes_in_kernel, xtab, yin, whole, (slabs, part, grid, grid), "planes_in")
        spectra.append(spec.reshape(slabs * part, grid, grid))
    out = None
    for c, (lo, part) in enumerate(zip(starts, PARTS)):
        spec = columns(ztab, spectra, c).reshape(slabs, part, grid, grid)
        back = planes(planes_out_kernel, xtab, yout, spec, (slabs, wides, part * rows, grid), "planes_out")
        piece = exchange(back.reshape(devices, part * rows, grid)).reshape(devices, part, rows, grid)
        out = join(piece, out, lo, (devices, depth, rows, grid))
    return out


def solution(mesh):
    placed = (P(None, "slab", "wide", None), P())
    return jax.shard_map(
        per_device,
        mesh=mesh,
        in_specs=placed,
        out_specs=P(None, "slab", "wide", None),
        check_vma=False,
    )
```

```python
import functools
import math

import jax
import jax.numpy as jnp
from jax import lax
from jax.experimental import pallas as pl
from jax.experimental.pallas import tpu as pltpu
from jax.sharding import PartitionSpec as P

AXES = ("slab", "wide")
HI = lax.Precision.HIGHEST
BLK = 128
PARTS = (16, 16)
SLOTS = 8
PANEL = 16


def hartley(length):
    index = jnp.arange(length, dtype=jnp.int32)
    phase = index[:, None] * index[None, :] % length
    angle = phase.astype(jnp.float32) * (2.0 * math.pi / length)
    return jnp.cos(angle) + jnp.sin(angle)


def exchange(blocks):
    return lax.all_to_all(blocks, AXES, split_axis=0, concat_axis=0, tiled=True)


def halves(value):
    top = value.astype(jnp.bfloat16)
    return top, (value - top.astype(jnp.float32)).astype(jnp.bfloat16)


def split(value):
    top = lax.reduce_precision(value, exponent_bits=8, mantissa_bits=7)
    return top.astype(jnp.bfloat16), (value - top).astype(jnp.bfloat16)


def mul3(left, right):
    def one(a, b):
        return jnp.dot(a, b, preferred_element_type=jnp.float32)

    return one(left[0], right[0]) + (one(left[1], right[0]) + one(left[0], right[1]))


def stacked3(left, right):
    size = left[0].shape[0]
    both = jnp.dot(jnp.concatenate(left, axis=0), right[0], preferred_element_type=jnp.float32)
    return both[:size] + (both[size:] + jnp.dot(left[0], right[1], preferred_element_type=jnp.float32))


def left3(high, low, value):
    top = jnp.concatenate([high, high], axis=1)
    bottom = jnp.concatenate([low, jnp.zeros_like(low)], axis=1)
    table = jnp.concatenate([top, bottom], axis=0)
    both = jnp.dot(table, jnp.concatenate(halves(value), axis=0), preferred_element_type=jnp.float32)
    return both[: high.shape[0]] + both[high.shape[0] :]


def whole_spec():
    return pl.BlockSpec(memory_space=pltpu.VMEM)


def pick_kernel(info, orb, out_ref, buf, acc, order, sems):
    npoint = info.shape[1]
    lane = lax.broadcasted_iota(jnp.int32, (acc.shape[0], BLK), 1)

    def collect(m, count):
        order[count] = m
        return count + info[0, m]

    total = lax.fori_loop(0, npoint, collect, 0, unroll=16)

    def copy(i):
        m = order[i]
        slot = i % SLOTS
        return pltpu.make_async_copy(orb.at[:, info[1, m]], buf.at[slot], sems.at[slot])

    @pl.loop(0, jnp.minimum(total, SLOTS - 1))
    def _(i):
        copy(i).start()

    acc[...] = jnp.zeros_like(acc)

    @pl.loop(0, total)
    def _(i):
        @pl.when(i + SLOTS - 1 < total)
        def _():
            copy(i + SLOTS - 1).start()

        copy(i).wait()
        m = order[i]
        slot = i % SLOTS
        line = buf[slot, :, info[2, m], :]
        moved = pltpu.roll(line, (m + BLK - info[3, m]) % BLK, 1)
        spot = pl.multiple_of(m // BLK * BLK, BLK)
        acc[:, pl.ds(spot, BLK)] = jnp.where(lane == m % BLK, moved, acc[:, pl.ds(spot, BLK)])

    out_ref[...] = acc[...].T


def pick(info, orbitals):
    norbit, depth, rows, grid = orbitals.shape
    npoint = info.shape[1]
    return pl.pallas_call(
        pick_kernel,
        out_shape=jax.ShapeDtypeStruct((npoint, norbit), jnp.float32),
        in_specs=[pl.BlockSpec(memory_space=pltpu.SMEM), pl.BlockSpec(memory_space=pl.ANY)],
        out_specs=whole_spec(),
        scratch_shapes=[
            pltpu.VMEM((SLOTS, norbit, rows, grid), jnp.float32),
            pltpu.VMEM((norbit, npoint), jnp.float32),
            pltpu.SMEM((npoint + 1,), jnp.int32),
            pltpu.SemaphoreType.DMA((SLOTS,)),
        ],
        name="pick",
    )(info, orbitals)


def factor_block(tile):
    lane = lax.broadcasted_iota(jnp.int32, (8, BLK), 1)
    sub = lax.broadcasted_iota(jnp.int32, (8, BLK), 0)
    cur = tile
    done, invs = [], []
    for p in range(BLK // PANEL):
        lo = PANEL * p
        inside = (lane >= lo) & (lane < lo + PANEL)
        E = {}
        for i0 in range(0, PANEL, 8):
            R = cur[i0:i0 + 8, :]
            for j in range(min(PANEL, i0 + 8)):
                cj = jnp.broadcast_to(R[:, lo + j : lo + j + 1], (8, BLK))
                for i in range(max(j, i0), i0 + 8):
                    E[i, j] = jnp.broadcast_to(cj[i - i0 : i - i0 + 1, :], (8, BLK))
        rows = [jnp.where(inside, jnp.where(lane == lo + k, 1.0, 0.0), jnp.broadcast_to(cur[k : k + 1, :], (8, BLK))) for k in range(PANEL)]
        U = [jnp.zeros((8, BLK), jnp.float32)] * (PANEL // 8); I = list(U)
        for k in range(PANEL):
            inv = 1.0 / E[k, k]
            g = k // 8
            U[g] = jnp.where(sub == k - 8 * g, rows[k], U[g])
            I[g] = jnp.where(sub == k - 8 * g, inv, I[g])
            ls = {i: E[i, k] * inv for i in range(k + 1, PANEL)}
            for i in range(k + 1, PANEL):
                for j in range(k + 1, i + 1):
                    E[i, j] = E[i, j] - ls[i] * E[j, k]
                rows[i] = rows[i] - ls[i] * rows[k]
        Uc = jnp.concatenate(U, axis=0); Ic = jnp.concatenate(I, axis=0)
        done.append(Uc); invs.append(Ic)
        if p < BLK // PANEL - 1:
            upd = lax.dot_general(Uc, Uc * Ic, (((0,), (0,)), ((), ())), precision=HI, preferred_element_type=jnp.float32)
            rest = cur[PANEL:, :]
            lanes = lax.broadcasted_iota(jnp.int32, rest.shape, 1)
            cur = jnp.where((lanes >= lo) & (lanes < lo + PANEL), 0.0, rest) - upd[lo + PANEL :, :]
    return jnp.concatenate(done, axis=0), jnp.concatenate(invs, axis=0)


def coeff_kernel(s_ref, ch_ref, cl_ref, sh_ref, sl_ref, out_ref, g_ref, p_ref, l_ref):
    n = s_ref.shape[0]
    nb = n // BLK
    rows = s_ref[...]
    sh_ref[...], sl_ref[...] = halves(rows)
    corr = lax.dot_general(rows, rows, (((1,), (1,)), ((), ())), precision=HI, preferred_element_type=jnp.float32)
    gram = corr * corr
    r = lax.broadcasted_iota(jnp.int32, (n, n), 0)
    c = lax.broadcasted_iota(jnp.int32, (n, n), 1)
    mean = jnp.sum(jnp.where(r == c, gram, 0.0)) * (1.0 / n)
    g_ref[...] = gram + jnp.where(r == c, 0.01 * mean, 0.0)
    rr = lax.broadcasted_iota(jnp.int32, (BLK, BLK), 0)
    cc = lax.broadcasted_iota(jnp.int32, (BLK, BLK), 1)

    def step(t, carry):
        start = pl.multiple_of((nb - 1 - t) * BLK, BLK)
        tile, invs = factor_block(g_ref[pl.ds(start, BLK), pl.ds(start, BLK)])
        low = jnp.where(cc <= rr, tile, 0.0) * jnp.sqrt(invs)
        l_ref[pl.ds(start, BLK), :] = low
        panel = jnp.dot(low, g_ref[pl.ds(start, BLK), :], precision=HI, preferred_element_type=jnp.float32)
        p_ref[pl.ds(start, BLK), :] = panel

        @pl.when(t < nb - 1)
        def _():
            g_ref[...] -= lax.dot_general(panel, panel, (((0,), (0,)), ((), ())), precision=HI, preferred_element_type=jnp.float32)
        return carry

    lax.fori_loop(0, nb, step, 0)
    first = l_ref[0:BLK, :]
    out_ref[:, 0:BLK] = lax.dot_general(first, first, (((0,), (0,)), ((), ())), precision=HI, preferred_element_type=jnp.float32)
    for b in range(1, nb):
        lo = b * BLK
        part = lax.dot_general(out_ref[:, 0:lo], p_ref[lo : lo + BLK, 0:lo], (((1,), (1,)), ((), ())), precision=HI, preferred_element_type=jnp.float32)
        out_ref[:, lo : lo + BLK] = -jnp.dot(part, l_ref[lo : lo + BLK, :], precision=HI, preferred_element_type=jnp.float32)
    ch_ref[...], cl_ref[...] = halves(out_ref[...])


def coefficients(rows):
    n, width = rows.shape
    coeff = jax.ShapeDtypeStruct((BLK, n), jnp.bfloat16)
    sample = jax.ShapeDtypeStruct((n, width), jnp.bfloat16)
    ch, cl, sh, sl = pl.pallas_call(
        coeff_kernel,
        out_shape=[coeff, coeff, sample, sample],
        scratch_shapes=[
            pltpu.VMEM((BLK, n), jnp.float32),
            pltpu.VMEM((n, n), jnp.float32),
            pltpu.VMEM((n, n), jnp.float32),
            pltpu.VMEM((n, BLK), jnp.float32),
        ],
        name="coefficients",
    )(rows)
    return (ch, cl), (sh, sl)


def fit_kernel(sh, sl, ch, cl, orb, out_ref, bh, bl):
    lines = orb.shape[1]
    turned = jnp.transpose(orb[...], (1, 0, 2))
    for r in range(lines):
        top, low = halves(turned[r])
        bh[:, r * BLK : (r + 1) * BLK] = top
        bl[:, r * BLK : (r + 1) * BLK] = low
    pairs = stacked3((sh[...], sl[...]), (bh[...], bl[...]))
    piece = stacked3((ch[...], cl[...]), halves(pairs * pairs))
    piece = jnp.stack([piece[:, r * BLK : (r + 1) * BLK] for r in range(lines)], axis=0)
    out_ref[...] = jnp.transpose(piece, (1, 0, 2))


def fit(sampled, coeffs, orbitals, first, count, lines=8):
    norbit, total, grid = orbitals.shape
    vectors, npoint = coeffs[0].shape
    start = first // lines
    return pl.pallas_call(
        fit_kernel,
        out_shape=jax.ShapeDtypeStruct((vectors, count, grid), jnp.float32),
        grid=(count // lines,),
        in_specs=[
            pl.BlockSpec((npoint, norbit), lambda i: (0, 0)),
            pl.BlockSpec((npoint, norbit), lambda i: (0, 0)),
            pl.BlockSpec((vectors, npoint), lambda i: (0, 0)),
            pl.BlockSpec((vectors, npoint), lambda i: (0, 0)),
            pl.BlockSpec((norbit, lines, grid), lambda i: (0, start + i, 0)),
        ],
        out_specs=pl.BlockSpec((vectors, lines, grid), lambda i: (0, i, 0)),
        scratch_shapes=[
            pltpu.VMEM((norbit, lines * grid), jnp.bfloat16),
            pltpu.VMEM((norbit, lines * grid), jnp.bfloat16),
        ],
        cost_estimate=pl.CostEstimate(
            flops=6 * count * grid * npoint * (norbit + vectors),
            transcendentals=0,
            bytes_accessed=4 * count * grid * (norbit + vectors),
        ),
        name="fit",
    )(*sampled, *coeffs, orbitals)


def planes_in_kernel(xh, xl, yh, yl, in_ref, out_ref):
    pairs = in_ref.shape[2] // 8
    group = pairs // 2
    for p in range(0, pairs, group):
        tall = [in_ref[0, :, 8 * (p + g) : 8 * (p + g) + 8, :].reshape(2 * BLK, BLK) for g in range(group)]
        along = mul3(halves(jnp.concatenate(tall, axis=0)), (xh[...], xl[...]))
        wide = [along[2 * BLK * g : 2 * BLK * (g + 1)] for g in range(group)]
        both = mul3((yh[...], yl[...]), halves(jnp.concatenate(wide, axis=1)))
        for g in range(group):
            out_ref[0, 2 * (p + g)] = both[:BLK, BLK * g : BLK * (g + 1)]
            out_ref[0, 2 * (p + g) + 1] = both[BLK:, BLK * g : BLK * (g + 1)]


def planes_out_kernel(xh, xl, yh, yl, in_ref, out_ref):
    pairs = in_ref.shape[1] // 2
    wide = [in_ref[0, 2 * g : 2 * g + 2].reshape(2 * BLK, BLK) for g in range(pairs)]
    both = mul3((yh[...], yl[...]), halves(jnp.concatenate(wide, axis=1)))
    tall = [both[:, BLK * g : BLK * (g + 1)] for g in range(pairs)]
    along = mul3(halves(jnp.concatenate(tall, axis=0)), (xh[...], xl[...]))
    for g in range(pairs):
        out_ref[0, :, 8 * g : 8 * g + 8, :] = along[2 * BLK * g : 2 * BLK * (g + 1)].reshape(32, 8, BLK)


def planes(kernel, xtab, ytab, values, out_shape, name):
    inward = name == "planes_in"
    slabs, depth = (values.shape[0], values.shape[2] // 4) if inward else values.shape[:2]
    cellwise = pl.BlockSpec((1, 32, 4 * depth, BLK), lambda s: (s, 0, 0, 0))
    planewise = pl.BlockSpec((1, depth, BLK, BLK), lambda s: (s, 0, 0, 0))
    small = pl.BlockSpec((BLK, BLK), lambda s: (0, 0))
    large = pl.BlockSpec((2 * BLK, 2 * BLK), lambda s: (0, 0))
    return pl.pallas_call(
        kernel,
        out_shape=jax.ShapeDtypeStruct(out_shape, jnp.float32),
        grid=(slabs,),
        in_specs=[small, small, large, large, cellwise if inward else planewise],
        out_specs=planewise if inward else cellwise,
        cost_estimate=pl.CostEstimate(
            flops=6 * values.size * 3 * BLK, transcendentals=0, bytes_accessed=8 * values.size
        ),
        name=name,
    )(*xtab, *ytab, values)


def columns_kernel(start, zh, zl, *refs):
    ins, out = refs[:-1], refs[-1]
    lines = ins[0].shape[1]
    base = pl.program_id(0) * lines
    length = BLK
    unit = 2.0 * math.pi / length

    def square(index):
        signed = jnp.where(index > length // 2, index - length, index).astype(jnp.float32) * unit
        return signed * signed

    zsq = square(lax.broadcasted_iota(jnp.int32, (BLK, BLK), 0))
    xsq = square(lax.broadcasted_iota(jnp.int32, (BLK, BLK), 1))
    flat = zsq + xsq
    tile = jnp.concatenate([jnp.transpose(ref[...], (1, 0, 2)) for ref in ins], axis=1)
    spec = left3(zh[0], zl[0], jnp.concatenate([tile[j] for j in range(lines)], axis=1))
    scale = 4.0 * math.pi / float(length**3)
    weights = []
    for j in range(lines):
        total = flat + square(jnp.full((BLK, BLK), base + j, jnp.int32))
        safe = jnp.where(total > 0, total, 1.0)
        weights.append(jnp.where(total > 0, scale / safe, 0.0))
    spec = spec * jnp.concatenate(weights, axis=1)
    part = out.shape[0]
    back = left3(zh[1, start : start + part], zl[1, start : start + part], spec)
    back = jnp.stack([back[:, j * BLK : (j + 1) * BLK] for j in range(lines)], axis=0)
    out[...] = jnp.transpose(back, (1, 0, 2))


def columns(ztab, values, which, lines=16):
    start = sum(v.shape[0] for v in values[:which])
    specs = [pl.BlockSpec((v.shape[0], lines, BLK), lambda i: (0, i, 0)) for v in values]
    table = pl.BlockSpec((2, BLK, BLK), lambda i: (0, 0, 0))
    size = BLK**3
    return pl.pallas_call(
        functools.partial(columns_kernel, start),
        out_shape=jax.ShapeDtypeStruct(values[which].shape, jnp.float32),
        grid=(BLK // lines,),
        in_specs=[table, table] + specs,
        out_specs=specs[which],
        cost_estimate=pl.CostEstimate(flops=9 * size * BLK, transcendentals=size, bytes_accessed=6 * size),
        name="columns",
    )(*ztab, *values)


def join_kernel(first, src, *refs):
    out, sems = refs[-2], refs[-1]
    quarter = src.shape[0] // 4
    copies = [
        pltpu.make_async_copy(
            src.at[pl.ds(k * quarter, quarter)],
            out.at[pl.ds(k * quarter, quarter), pl.ds(first, src.shape[1])],
            sems.at[k],
        )
        for k in range(4)
    ]
    for copy in copies:
        copy.start()
    for copy in copies:
        copy.wait()


def join(piece, whole, first, shape):
    anywhere = pl.BlockSpec(memory_space=pl.ANY)
    args = (piece,) if whole is None else (piece, whole)
    return pl.pallas_call(
        functools.partial(join_kernel, first),
        out_shape=jax.ShapeDtypeStruct(shape, jnp.float32),
        in_specs=[whole_spec()] + [anywhere] * (len(args) - 1),
        out_specs=anywhere,
        input_output_aliases={} if whole is None else {1: 0},
        scratch_shapes=[pltpu.SemaphoreType.DMA((4,))],
        cost_estimate=pl.CostEstimate(flops=0, transcendentals=0, bytes_accessed=8 * piece.size),
        name="join",
    )(*args)


def per_device(orbitals, points):
    norbit, depth, rows, grid = orbitals.shape
    npoint = points.shape[0]
    slabs = lax.axis_size("slab")
    wides = lax.axis_size("wide")
    slab_index = lax.axis_index("slab")
    wide_index = lax.axis_index("wide")
    devices = slabs * wides
    zcoord = points // (grid * grid)
    ycoord = points // grid % grid
    xcoord = points % grid
    owned = (zcoord // depth == slab_index) & (ycoord // rows == wide_index)
    info = jnp.stack([owned.astype(jnp.int32), zcoord % depth, ycoord % rows, xcoord])
    picked = pick(info, orbitals)
    mine = exchange(picked.reshape(devices, npoint // devices, norbit)).sum(0)
    sampled_rows = exchange(jnp.broadcast_to(mine[None], (devices,) + mine.shape))
    sampled_rows = sampled_rows.reshape(npoint, norbit)
    coeffs, sampled = coefficients(sampled_rows)
    table = hartley(grid)
    xtab = split(table)
    lines = table.reshape(grid, wides, 1, rows)
    eye = jnp.eye(2, dtype=jnp.float32)
    ysplit = (eye[:, None, None, :, None] * lines[None]).reshape(2 * grid, wides * 2 * rows)
    starts = [sum(PARTS[:c]) for c in range(len(PARTS))]
    zrows = table.reshape(grid, slabs, depth)
    ztable = jnp.concatenate(
        [zrows[:, :, lo : lo + part].reshape(grid, slabs * part) for lo, part in zip(starts, PARTS)], axis=1
    )
    yin, yout = split(ysplit), split(ysplit.T)
    ztab = split(jnp.stack([ztable, ztable.T]))

    flat = orbitals.reshape(norbit, depth * rows, grid)
    spectra = []
    for lo, part in zip(starts, PARTS):
        piece = fit(sampled, coeffs, flat, lo * rows, part * rows)
        piece, flat = lax.optimization_barrier((piece, flat))
        whole = exchange(piece).reshape(slabs, wides, part * rows, grid)
        spec = planes(planes_in_kernel, xtab, yin, whole, (slabs, part, grid, grid), "planes_in")
        spectra.append(spec.reshape(slabs * part, grid, grid))
    out = None
    for c, (lo, part) in enumerate(zip(starts, PARTS)):
        spec = columns(ztab, spectra, c).reshape(slabs, part, grid, grid)
        back = planes(planes_out_kernel, xtab, yout, spec, (slabs, wides, part * rows, grid), "planes_out")
        piece = exchange(back.reshape(devices, part * rows, grid)).reshape(devices, part, rows, grid)
        out = join(piece, out, lo, (devices, depth, rows, grid))
    return out


def solution(mesh):
    placed = (P(None, "slab", "wide", None), P())
    return jax.shard_map(
        per_device,
        mesh=mesh,
        in_specs=placed,
        out_specs=P(None, "slab", "wide", None),
        check_vma=False,
    )
```
